256 devices in a mesh: frame: 8 (over z_hi, core), fsdp: 32 (over x, z_lo, y).
Axes of the slice: x: 4, y: 4, z: 8 (z_hi: 4, z_lo: 2; z = z_hi * 2 + z_lo), core: 2. Of those that a mesh axis runs over, the one named last changes fastest.
Arguments:
- window: bfloat16 [8, 512, 5120], P('frame', 'fsdp'), may hold values from -6 to 6
- levels: int32 [8], P('frame'), may hold values from 0 to 15
- actions: int32 [8], P('frame'), may hold values from 0 to 15
- cache_len: int32 [1], replicated, may hold values from 512 to 15872
- level_table: float32 [16, 3, 5120], replicated, may hold values from -4 to 4
- action_table: float32 [16, 3, 5120], replicated, may hold values from -4 to 4
- w_qkv: bfloat16 [3, 5120, 4096], P(None, None, 'fsdp'), may hold values from -0.078125 to 0.078125
- w_out: bfloat16 [4096, 5120], P('fsdp'), may hold values from -0.09375 to 0.09375
- cache_keys: bfloat16 [16384, 4096], P('frame', 'fsdp'), may hold values from -220 to 220
- cache_values: bfloat16 [16384, 4096], P('frame', 'fsdp'), may hold values from -6 to 6
- fresh_frame: bfloat16 [512, 5120], P('fsdp'), may hold values from -6 to 6
Outputs:
- next_window: bfloat16 [8, 512, 5120], P('frame', 'fsdp')
- finished: bfloat16 [512, 5120], P('fsdp')
- new_cache_keys: bfloat16 [16384, 4096], P('frame', 'fsdp')
- new_cache_values: bfloat16 [16384, 4096], P('frame', 'fsdp')
The draws below stay inside these ranges and needn't reach their ends.
Inputs may be any that keep to these rules, and one draw needn't show every extreme that they name: Rows of the cache from cache_len on are unused.
All inputs are finite; a program needn't handle non-finite values.
Results may differ from the reference program's by a relative error of at most 0.015.
The reference program's roundings to bfloat16 on the way (of `normed`, `attended` and `updated`) count: a program that leaves them out, or rounds other values in their place, can miss the bound.
Values may be sent and summed in bfloat16 or wider, within the bound.
No kernel may reach another device: no remote copies, remote signals or barrier semaphores. Data moves between devices by JAX's collectives and lax.ppermute only.
A program may use at most 128 MiB of HBM per device.

```python
import math
import jax
import jax.numpy as jnp
from jax import lax

D = 5120
H = 32
HD = 128
LEVELS = 16
ACTIONS = 16
WINDOW = 8
FT = 512
CACHE = 16384


def draw_cache_keys(key, part):
    shape = (CACHE, H * HD)
    result = jnp.clip(jax.random.normal(key, shape, jnp.float32), -6.0, 6.0)
    return result.astype(jnp.bfloat16)


def place_ends(drawn, rng, low, high):
    extent = drawn.shape
    place = [jax.random.randint(jax.random.fold_in(rng, axis), (), 0, extent[axis]) for axis in range(len(extent))]
    drawn = drawn.at[tuple(place)].set(low)
    longest = extent.index(max(extent))
    place[longest] = (place[longest] + 1) % extent[longest]
    return drawn.at[tuple(place)].set(high)


def shard_levels(stream_key, dims, split, smallest, high):
    gain = 1.0
    for dim, shards_of in split:
        heights = jax.random.uniform(jax.random.fold_in(jax.random.fold_in(stream_key, 6), dim), (shards_of,), jnp.float32, smallest / len(split), high / len(split))
        gain = gain * jnp.repeat(jnp.exp(heights), dims[dim] // shards_of).reshape((-1,) + (1,) * (len(dims) - 1 - dim))
    return gain


def bell_draw(rng, extent, scale, most, pieces=(), kind=jnp.bfloat16):
    loudness = shard_levels(rng, extent, pieces, -0.22, 0.18) if pieces else 1.0
    values = jax.random.normal(rng, extent, jnp.float32) * scale * loudness
    return jnp.minimum(jnp.maximum(values, -most), most).astype(kind)


def setup_inputs(seed: int = 0) -> dict:
    seeds = jax.random.split(jax.random.key(seed), 12)
    window = bell_draw(seeds[0], (WINDOW, FT, D), 1.0, 6.0, ((0, 8), (1, 32)))
    levels = place_ends(jax.random.randint(seeds[1], (WINDOW,), 0, LEVELS), jax.random.fold_in(seeds[1], 1), 0, LEVELS - 1).astype(jnp.int32)
    actions = place_ends(jax.random.randint(seeds[2], (WINDOW,), 0, ACTIONS), jax.random.fold_in(seeds[2], 1), 0, ACTIONS - 1).astype(jnp.int32)
    cache_len = jax.random.randint(seeds[3], (1,), FT, CACHE - FT + 1).astype(jnp.int32)
    level_table = bell_draw(seeds[4], (LEVELS, 3, D), 0.7, 4.0, (), jnp.float32)
    action_table = bell_draw(seeds[5], (ACTIONS, 3, D), 0.7, 4.0, (), jnp.float32)
    w_qkv = bell_draw(seeds[6], (3, D, H * HD), D ** -0.5, 0.078125, ((2, 32),))
    w_out = bell_draw(seeds[7], (H * HD, D), (H * HD) ** -0.5, 0.09375, ((0, 32),))
    cache_keys = draw_cache_keys(jax.random.fold_in(seeds[11], 71), 0)
    cache_values = bell_draw(seeds[9], (CACHE, H * HD), 1.0, 6.0, ((0, 8), (1, 32)))
    fresh_frame = bell_draw(seeds[10], (FT, D), 1.0, 6.0, ((0, 32),))
    return {"window": window, "levels": levels, "actions": actions, "cache_len": cache_len, "level_table": level_table, "action_table": action_table, "w_qkv": w_qkv, "w_out": w_out, "cache_keys": cache_keys, "cache_values": cache_values, "fresh_frame": fresh_frame}


EPS = 1e-06
NEG = -1e+30

def reference(window, levels, actions, cache_len, level_table, action_table, w_qkv, w_out, cache_keys, cache_values, fresh_frame):
    condition = level_table[levels] + action_table[actions]
    shift = condition[:, 0][:, None, :]
    scale = condition[:, 1][:, None, :]
    gate = condition[:, 2][:, None, :]
    base_rows = window.astype(jnp.float32)
    center = base_rows - lax.optimization_barrier(jnp.mean(base_rows, axis=-1, keepdims=True))
    spread = lax.optimization_barrier(jnp.mean(center * center, axis=-1, keepdims=True))
    normed = (center * lax.rsqrt(spread + EPS) * (1.0 + scale) + shift).astype(jnp.bfloat16)
    flat = normed.reshape(WINDOW * FT, D)
    projected = [jnp.dot(flat, w_qkv[index], preferred_element_type=jnp.float32).astype(jnp.bfloat16) for index in range(3)]
    query, key, value = [item.reshape(WINDOW, FT, H, HD).transpose(2, 0, 1, 3) for item in projected]
    past_keys = cache_keys.reshape(CACHE, H, HD).transpose(1, 0, 2)
    past_values = cache_values.reshape(CACHE, H, HD).transpose(1, 0, 2)
    length = cache_len[0]
    past_valid = jnp.arange(CACHE, dtype=jnp.int32) < length
    factor = 1.0 / math.sqrt(HD)

    def one_head(inputs):
        queries, keys_now, values_now, keys_past, values_past = inputs
        all_keys = jnp.concatenate([keys_past, keys_now.reshape(WINDOW * FT, HD)], 0)
        all_values = jnp.concatenate([values_past, values_now.reshape(WINDOW * FT, HD)], 0)
        results = []
        for frame in range(WINDOW):
            valid = jnp.concatenate([past_valid, jnp.repeat(jnp.arange(WINDOW) <= frame, FT)])
            scores = jnp.dot(queries[frame], all_keys.T, preferred_element_type=jnp.float32) * factor
            scores = jnp.where(valid[None, :], scores, NEG)
            peak = lax.optimization_barrier(jnp.max(scores, axis=-1, keepdims=True))
            weights = jnp.where(valid[None, :], jnp.exp(scores - peak), 0.0)
            total = lax.optimization_barrier(jnp.sum(weights, axis=-1, keepdims=True))
            mixed = jnp.dot(weights.astype(jnp.bfloat16), all_values, preferred_element_type=jnp.float32) / total
            results.append(mixed.astype(jnp.bfloat16))
        return jnp.stack(results)
    heads = lax.map(one_head, (query, key, value, past_keys, past_values))
    attended = heads.transpose(1, 2, 0, 3).reshape(WINDOW * FT, H * HD)
    projection = jnp.dot(attended, w_out, preferred_element_type=jnp.float32).reshape(WINDOW, FT, D)
    updated = (base_rows + gate * projection).astype(jnp.bfloat16)
    next_window = jnp.concatenate([updated[1:], fresh_frame[None]], 0)
    finished = updated[0]
    first_keys = key[:, 0].transpose(1, 0, 2).reshape(FT, H * HD)
    first_values = value[:, 0].transpose(1, 0, 2).reshape(FT, H * HD)
    start = length.astype(jnp.int32)
    zero = jnp.zeros((), jnp.int32)
    new_cache_keys = lax.dynamic_update_slice(cache_keys, first_keys, (start, zero))
    new_cache_values = lax.dynamic_update_slice(cache_values, first_values, (start, zero))
    return (next_window, finished, new_cache_keys, new_cache_values)
```

```python
import math

import jax
import jax.numpy as jnp
from jax import lax
from jax.experimental import pallas as pl
from jax.experimental.pallas import tpu as pltpu
from jax.sharding import Mesh
from jax.sharding import PartitionSpec as P

HD = 128
D = 5120
FT = 512
TOK = 16
PARTS = 5
PW = D // PARTS
EPS = 1e-06
NEG = -1e30
LOG2E = math.log2(math.e)
EXP_SCALE = LOG2E / math.sqrt(HD)
CHUNK = 1024
PAY = FT + 16

FRAME = ("zh", "core")
FSDP = ("x", "zl", "y")


DIMS = (("x", 1, 4), ("x", 3, 4), ("zl", 1, 2), ("y", 1, 4), ("y", 3, 4))


def across(block, dim):
    axis, mask, size = DIMS[dim]
    return lax.ppermute(block, axis, [(i, i ^ mask) for i in range(size)])


def frame_shift(block, distance):
    return lax.ppermute(block, FRAME, [(i, (i + distance) % 8) for i in range(8)])


def other_core(block):
    return lax.ppermute(block, "core", [(0, 1), (1, 0)])


def norm_body(window_ref, condition_ref, *outs):
    rows = window_ref[0].astype(jnp.float32)
    center = rows - jnp.mean(rows, axis=-1, keepdims=True)
    spread = jnp.mean(center * center, axis=-1, keepdims=True)
    normed = (
        center * lax.rsqrt(spread + EPS) * (1.0 + condition_ref[1:2, :]) + condition_ref[0:1, :]
    ).astype(jnp.bfloat16)
    for p in range(PARTS):
        outs[p][...] = normed[:, p * PW : (p + 1) * PW]


def normalise(window, condition):
    return pl.pallas_call(
        norm_body,
        out_shape=[jax.ShapeDtypeStruct((TOK, PW), jnp.bfloat16)] * PARTS,
        name="normalise",
    )(window, condition)


def merge_body(*refs):
    for p in range(PARTS):
        rows = refs[p].shape[0]
        refs[2 * PARTS + p][:rows, :] = refs[p][...]
        refs[2 * PARTS + p][rows:, :] = refs[PARTS + p][...]


def merge(held, got):
    rows = held[0].shape[0]
    return pl.pallas_call(
        merge_body,
        out_shape=[jax.ShapeDtypeStruct((2 * rows, PW), jnp.bfloat16)] * PARTS,
        name="merge",
    )(*held, *got)


def after(block, *earlier):
    return lax.optimization_barrier((block, *earlier))[0]


def canonical(part, index, last):
    bits = 0
    for s in range(4):
        if (index >> s) & 1:
            bits |= 16 >> ((part + s) % PARTS)
    if last:
        bits |= 16 >> ((part + 4) % PARTS)
    return bits


def qkv_first(*refs):
    parts, w_ref, acc_ref = refs[:PARTS], refs[PARTS], refs[PARTS + 1]
    acc_ref[...] = jnp.zeros(acc_ref.shape, jnp.float32)
    qkv_add(parts, w_ref, acc_ref, False)


def qkv_add(parts, w_ref, acc_ref, last):
    for p in range(PARTS):
        w = jnp.concatenate([w_ref[c, p * PW : (p + 1) * PW, :] for c in range(3)], axis=1)
        product = jnp.dot(parts[p][...], w, preferred_element_type=jnp.float32)
        for j in range(16):
            r = canonical(p, j, last) * TOK
            acc_ref[r : r + TOK, :] += product[j * TOK : (j + 1) * TOK, :]


def qkv_last(*refs):
    parts, w_ref, before_ref = refs[:PARTS], refs[PARTS], refs[PARTS + 1]
    outs, acc_ref = refs[PARTS + 2 : PARTS + 4], refs[PARTS + 4]
    acc_ref[...] = before_ref[...]
    qkv_add(parts, w_ref, acc_ref, True)
    outs[0][...] = acc_ref[:, :HD].astype(jnp.bfloat16)
    outs[1][...] = acc_ref[:, HD:].astype(jnp.bfloat16)


def project(mine, theirs, w_qkv):
    acc = pl.pallas_call(
        qkv_first,
        out_shape=jax.ShapeDtypeStruct((FT, 3 * HD), jnp.float32),
        name="qkv_first",
    )(*mine, w_qkv)
    return pl.pallas_call(
        qkv_last,
        out_shape=[
            jax.ShapeDtypeStruct((FT, HD), jnp.bfloat16),
            jax.ShapeDtypeStruct((FT, 2 * HD), jnp.bfloat16),
        ],
        scratch_shapes=[pltpu.VMEM((FT, 3 * HD), jnp.float32)],
        name="qkv_last",
    )(*theirs, w_qkv, acc)


def attention_body(limits, q_ref, k0, v0, k1, v1, kv0, kv1, o_ref, stat_ref):
    chunks = []
    for c, (k, v) in enumerate(((k0, v0), (k1, v1))):
        for at in range(0, k.shape[0], CHUNK):
            chunks.append((k, v, 0, 0, at, min(CHUNK, k.shape[0] - at), limits[c] - at))
    for c, kv in enumerate((kv0, kv1)):
        chunks.append((kv, kv, 0, HD, 0, FT, limits[2 + c]))
    any_key = (limits[0] > 0) | (limits[1] > 0) | (limits[2] > 0) | (limits[3] > 0)
    rows = 256
    ones = jnp.ones((CHUNK, HD), jnp.bfloat16)

    def one_block(index, carry):
        start = pl.multiple_of(index * rows, rows)
        q = q_ref[pl.ds(start, rows), :]
        peak = jnp.full((rows, 1), NEG, jnp.float32)
        acc = jnp.zeros((rows, 2 * HD), jnp.float32)
        for k, v, kc, vc, at, size, limit in chunks:
            s = lax.dot_general(
                q,
                k[at : at + size, kc : kc + HD],
                (((1,), (1,)), ((), ())),
                preferred_element_type=jnp.float32,
            )
            inside = lax.broadcasted_iota(jnp.int32, (1, size), 1) < limit
            s = jnp.where(inside, s, NEG)
            newest = jnp.maximum(peak, jnp.max(s, axis=-1, keepdims=True))
            w = jnp.exp2((s - newest) * EXP_SCALE).astype(jnp.bfloat16)
            values = jnp.concatenate([v[at : at + size, vc : vc + HD], ones[:size]], axis=1)
            acc = acc * jnp.exp2((peak - newest) * EXP_SCALE) + jnp.dot(
                w, values, preferred_element_type=jnp.float32
            )
            peak = newest
        total = acc[:, HD:]
        o_ref[pl.ds(start, rows), :] = jnp.where(any_key, acc[:, :HD] / total, 0.0).astype(
            jnp.bfloat16
        )
        level = jnp.where(any_key, peak * EXP_SCALE + jnp.log2(total), NEG)
        stat_ref[pl.ds(index, 1), :] = level.T[0:1, :]
        return carry

    lax.fori_loop(0, FT // rows, one_block, 0)
    flat = jnp.concatenate([stat_ref[i : i + 1, :] for i in range(FT // rows)], axis=1)
    high = flat.astype(jnp.bfloat16).astype(jnp.float32)
    rest = flat - high
    middle = rest.astype(jnp.bfloat16).astype(jnp.float32)
    low = rest - middle
    lines = []
    for piece in (high, middle, low):
        for at in range(0, FT, HD):
            lines.append(piece[:, at : at + HD])
    lines.append(jnp.zeros((4, HD), jnp.float32))
    o_ref[FT:, :] = jnp.concatenate(lines, axis=0).astype(jnp.bfloat16)


def attention(limits, q, k0, v0, k1, v1, kv0, kv1):
    whole = pl.BlockSpec(memory_space=pltpu.VMEM)
    return pl.pallas_call(
        attention_body,
        in_specs=[pl.BlockSpec(memory_space=pltpu.SMEM)] + [whole] * 7,
        out_shape=jax.ShapeDtypeStruct((PAY, HD), jnp.bfloat16),
        scratch_shapes=[pltpu.VMEM((8, 256), jnp.float32)],
        cost_estimate=pl.CostEstimate(
            flops=4 * FT * 5120 * HD, bytes_accessed=3 << 20, transcendentals=FT * 5120
        ),
        name="attention",
    )(limits, q, k0, v0, k1, v1, kv0, kv1)


def combine_body(*refs):
    parts, o_ref = refs[:-1], refs[-1]
    levels = []
    for part in parts:
        lines = part[FT:, :].astype(jnp.float32)
        level = (lines[0:4] + lines[4:8]) + lines[8:12]
        row = jnp.concatenate([level[i : i + 1, :] for i in range(4)], axis=1)
        levels.append(jnp.broadcast_to(row, (HD, FT)).T)
    peak = levels[0]
    for level in levels[1:]:
        peak = jnp.maximum(peak, level)
    total = jnp.zeros((FT, HD), jnp.float32)
    acc = jnp.zeros((FT, HD), jnp.float32)
    for part, level in zip(parts, levels):
        w = jnp.exp2(level - peak)
        total = total + w
        acc = acc + w * part[:FT, :].astype(jnp.float32)
    o_ref[...] = (acc / total).astype(jnp.bfloat16)


def combine(parts):
    return pl.pallas_call(
        combine_body,
        out_shape=jax.ShapeDtypeStruct((FT, HD), jnp.bfloat16),
        name="combine",
    )(*parts)


def insert_rows(shard, fresh_rows, first, length):
    shard_rows, width = shard.shape
    frame_tokens = fresh_rows.shape[0]
    offset = jnp.clip(length - first, -frame_tokens, shard_rows)
    padding = jnp.zeros((shard_rows, width), shard.dtype)
    padded = jnp.concatenate([padding, fresh_rows, padding], 0)
    placed = lax.dynamic_slice_in_dim(padded, shard_rows - offset, shard_rows, 0)
    position = first + jnp.arange(shard_rows, dtype=jnp.int32)
    inside = (position >= length) & (position < length + frame_tokens)
    return jnp.where(inside[:, None], placed, shard)


def in_token_order(relative):
    width = relative.shape[-1]
    blocks = relative.reshape(2, 2, 2, 2, 2, TOK, width)

    def ring(blocks, axis, index):
        pieces = [
            lax.index_in_dim(lax.index_in_dim(blocks, a, axis, True), b, axis + 1, True)
            for a, b in ((0, 0), (1, 0), (1, 1), (0, 1))
        ]
        pieces = [p.reshape(p.shape[:axis] + (1,) + p.shape[axis + 2 :]) for p in pieces]
        stacked = jnp.concatenate(pieces, axis)
        low = jnp.concatenate([lax.slice_in_dim(stacked, i ^ 1, (i ^ 1) + 1, axis=axis) for i in range(4)], axis)
        stacked = jnp.where(index & 1 == 1, low, stacked)
        high = jnp.concatenate([lax.slice_in_dim(stacked, i ^ 2, (i ^ 2) + 1, axis=axis) for i in range(4)], axis)
        return jnp.where(index & 2 == 2, high, stacked)

    blocks = ring(blocks, 3, lax.axis_index("y"))
    blocks = jnp.where(lax.axis_index("zl") == 1, jnp.flip(blocks, 2), blocks)
    blocks = ring(blocks, 0, lax.axis_index("x"))
    return blocks.reshape(FT, width)


CUTS = (0, 1792, 3456, 5120)
RING = (2, 3, 4)
QUARTER = D // 4
ROWS = FT // 4


def split_rows(axis, bit):
    return [r * TOK for r in range(8) if (r >> (2 - axis)) & 1 == bit]


def out_body(*refs):
    tokens = jnp.concatenate([r[...] for r in refs[:4]], axis=1)
    quarters, keeps, sends, y_ref = refs[4:20], refs[20:23], refs[23:26], refs[26]
    for c in range(4):
        weights = jnp.concatenate([w[...] for w in quarters[4 * c : 4 * c + 4]], axis=0)
        y_ref[:, c * QUARTER : (c + 1) * QUARTER] = jnp.dot(
            tokens, weights, preferred_element_type=jnp.float32
        ).astype(jnp.bfloat16)
    for p in range(3):
        for bit, out in ((0, keeps[p]), (1, sends[p])):
            for i, r in enumerate(split_rows(p, bit)):
                out[i * TOK : (i + 1) * TOK, :] = y_ref[r : r + TOK, CUTS[p] : CUTS[p + 1]]


def out_project(tokens, quarters):
    widths = [CUTS[p + 1] - CUTS[p] for p in range(3)]
    shapes = [jax.ShapeDtypeStruct((ROWS // 2, w), jnp.bfloat16) for w in widths]
    outs = pl.pallas_call(
        out_body,
        out_shape=shapes + shapes,
        scratch_shapes=[pltpu.VMEM((ROWS, D), jnp.bfloat16)],
        name="out_project",
    )(*tokens, *quarters)
    return outs[:3], outs[3:]


def add_body(*refs):
    keeps, gots, next_keeps, next_sends = refs[:3], refs[3:6], refs[6:9], refs[9:]
    for p in range(3):
        total = keeps[p][...].astype(jnp.float32) + gots[p][...].astype(jnp.float32)
        if not next_sends:
            next_keeps[p][...] = total
            continue
        total = total.astype(jnp.bfloat16)
        left = [d for d in (0, 1, 2) if d != p] if total.shape[0] == 4 * TOK else []
        if left:
            axis = left.index((p + 1) % 3)
            blocks = [[r for r in range(4) if (r >> (1 - axis)) & 1 == bit] for bit in (0, 1)]
        else:
            blocks = [[0], [1]]
        for ids, out in zip(blocks, (next_keeps[p], next_sends[p])):
            for i, r in enumerate(ids):
                out[i * TOK : (i + 1) * TOK, :] = total[r * TOK : (r + 1) * TOK, :]


def add_up(keeps, gots):
    rows = keeps[0].shape[0] // 2
    if rows < TOK:
        shapes = [jax.ShapeDtypeStruct(k.shape, jnp.float32) for k in keeps]
    else:
        shapes = [jax.ShapeDtypeStruct((rows, k.shape[1]), jnp.bfloat16) for k in keeps] * 2
    outs = pl.pallas_call(add_body, out_shape=shapes, name="add_up")(*keeps, *gots)
    return outs[:3], outs[3:]


def on_device(
    window,
    levels,
    actions,
    cache_len,
    level_table,
    action_table,
    w_qkv,
    w_out,
    cache_keys,
    cache_values,
    fresh_frame,
):
    core = lax.axis_index("core")
    slot = lax.axis_index(FRAME)
    length = cache_len[0]
    shard_rows = cache_keys.shape[0]

    other_keys = other_core(cache_keys)
    other_values = other_core(cache_values)

    condition = (
        lax.dynamic_slice_in_dim(level_table, levels[0], 1, 0)
        + lax.dynamic_slice_in_dim(action_table, actions[0], 1, 0)
    )[0]
    normed = normalise(window, condition)

    held = list(normed)
    for step in range(4):
        got = [across(held[p], (p + step) % PARTS) for p in range(PARTS)]
        held = merge(held, got)
    last = [across(held[p], (p + 4) % PARTS) for p in range(PARTS)]

    base_next = frame_shift(after(window[0], held[0]), -1)
    gate_next = frame_shift(after(condition[2:3], held[0]), -1)

    query, key_value = project(held, last, w_qkv)

    q_up = frame_shift(query, -2)
    q_down = frame_shift(query, 2)
    other_key_value = other_core(key_value)

    half = D // 2
    w_late = after(w_out, query)
    own = [lax.dynamic_slice_in_dim(w_late, core * half + i * QUARTER, QUARTER, 1) for i in (0, 1)]
    own += [
        lax.dynamic_slice_in_dim(w_late, (1 - core) * half + i * QUARTER, QUARTER, 1) for i in (0, 1)
    ]
    a_1, a_3 = across(own[0], 0), across(own[0], 1)
    b_3, b_1 = across(own[1], 1), across(own[1], 0)

    def attend(q, ahead):
        frame = (slot + ahead) % 8
        partner = slot ^ 1
        limits = jnp.stack(
            [
                length - slot * shard_rows,
                length - partner * shard_rows,
                jnp.where(slot <= frame, FT, 0),
                jnp.where(partner <= frame, FT, 0),
            ]
        ).astype(jnp.int32)
        return attention(
            limits, q, cache_keys, cache_values, other_keys, other_values, key_value, other_key_value
        )

    part = attend(query, 0)
    part, q_up, q_down = lax.optimization_barrier((part, q_up, q_down))
    q_far = [frame_shift(q_up[: FT // 2], -2), frame_shift(q_down[FT // 2 :], 2)]
    sent = [frame_shift(part, -1)]
    part = attend(q_up, 2)
    sent.append(frame_shift(part, 1))
    part, q_down, a_1, a_3, b_1, b_3 = lax.optimization_barrier((part, q_down, a_1, a_3, b_1, b_3))
    a_2, b_2 = across(a_1, 1), across(b_3, 0)
    part = attend(q_down, 6)
    sent.append(frame_shift(part, -3))
    part, q_far, a_2, b_2 = lax.optimization_barrier((part, q_far, a_2, b_2))
    near = [[own[0], a_1, a_3, a_2], [own[1], b_1, b_3, b_2]]
    far = [[own[2 + i]] + [other_core(w) for w in near[i][1:]] for i in range(2)]
    part = attend(jnp.concatenate(q_far, 0), 4)
    sent.append(frame_shift(part, 3))

    def from_slot(block, zh, c):
        pieces = [block]
        for d in (1, 3, 2):
            pieces.append(lax.ppermute(block, FRAME, [(2 * zh + c, 2 * ((zh + d) % 4) + c)]))
        here = lax.axis_index("zh") == zh
        spread = jnp.where(here, block, pieces[1] + pieces[2] + pieces[3])
        beside = lax.ppermute(spread, "core", [(c, 1 - c)])
        return jnp.where(core == c, spread, beside)

    root = in_token_order(from_slot(after(key_value, part), 0, 0))
    first = slot * shard_rows
    new_keys = insert_rows(cache_keys, root[:, :HD], first, length)
    new_values = insert_rows(cache_values, root[:, HD:], first, length)

    attended = combine(sent).reshape(2, 2, ROWS, HD)

    beyond = lax.ppermute(attended[1, 1], "x", [(i, i ^ 2) for i in range(4)])
    together = [attended[0, 0], across(attended[1, 0], 0), across(attended[0, 1], 1), beyond]
    keeps, sends = out_project(together, near[0] + near[1] + far[0] + far[1])
    for step in range(3):
        gots = [across(sends[p], RING[(p + step) % 3]) for p in range(3)]
        keeps, sends = add_up(keeps, gots)
    summed = jnp.concatenate(keeps, -1)
    projection = jnp.where(
        core == 0, summed, jnp.concatenate([summed[:, half:], summed[:, :half]], 1)
    )
    updated = (base_next.astype(jnp.float32) + gate_next * projection).astype(jnp.bfloat16)
    next_window = jnp.where(slot == 7, fresh_frame, updated)
    finished = from_slot(updated, 3, 1)
    return (next_window[None], finished, new_keys, new_values)


def solution(mesh):
    split = Mesh(mesh.devices.reshape(4, 2, 4, 2, 4), FRAME + FSDP)
    return jax.shard_map(
        on_device,
        mesh=split,
        in_specs=(
            P(FRAME, FSDP, None),
            P(FRAME),
            P(FRAME),
            P(),
            P(),
            P(),
            P(None, None, FSDP),
            P(FSDP, None),
            P(FRAME, FSDP),
            P(FRAME, FSDP),
            P(FSDP, None),
        ),
        out_specs=(P(FRAME, FSDP, None), P(FSDP, None), P(FRAME, FSDP), P(FRAME, FSDP)),
        check_vma=False,
    )
```

```python
import math

import jax
import jax.numpy as jnp
from jax import lax
from jax.experimental import pallas as pl
from jax.experimental.pallas import tpu as pltpu
from jax.sharding import Mesh
from jax.sharding import PartitionSpec as P

HD = 128
D = 5120
HALF = D // 2
FT = 512
TOK = 16
PW = D // 4
ROWS = FT // 4
EPS = 1e-06
NEG = -1e30
LOG2E = math.log2(math.e)
EXP_SCALE = LOG2E / math.sqrt(HD)
CHUNK = 1024
PAY = FT + 16

FRAME = ("zh", "core")
FSDP = ("x", "zl", "y")


XA, XB, ZL, YA, YB = range(5)
DIMS = (("x", 1), ("x", 3), ("zl", 1), ("y", 1), ("y", 3))
SIZES = {"x": 4, "zl": 2, "y": 4}
BIT = (16, 8, 4, 2, 1)
ORDER = (XA, YA, XB, YB, ZL)
GATHER = [[[ORDER[(2 * core + p + step) % 5] for core in (0, 1)] for p in (0, 1)] for step in range(5)]
REDUCE = [[(ZL, YA, YB)[step], (YA, YB, ZL)[step]] for step in range(3)]
SPREAD = [[(XA, XB)[step], (XB, XA)[step]] for step in range(2)]


def across(block, by_core):
    pairs = []
    for core in range(2):
        axis, mask = DIMS[by_core[core]]
        for x in range(4):
            for zl in range(2):
                for y in range(4):
                    at = {"x": x, "zl": zl, "y": y}
                    to = dict(at, **{axis: at[axis] ^ mask})
                    flat = [((core * 4 + p["x"]) * 2 + p["zl"]) * 4 + p["y"] for p in (at, to)]
                    pairs.append(tuple(flat))
    return lax.ppermute(block, ("core", "x", "zl", "y"), pairs)


def frame_shift(block, distance):
    return lax.ppermute(block, FRAME, [(i, (i + distance) % 8) for i in range(8)])


def other_core(block):
    return lax.ppermute(block, "core", [(0, 1), (1, 0)])


def after(block, *earlier):
    return lax.optimization_barrier((block, *earlier))[0]


SCALARS = pl.BlockSpec(memory_space=pltpu.SMEM)
WHOLE = pl.BlockSpec(memory_space=pltpu.VMEM)


def norm_body(core_ref, window_ref, condition_ref, keep_ref, send_ref):
    rows = window_ref[0].astype(jnp.float32)
    center = rows - jnp.mean(rows, axis=-1, keepdims=True)
    spread = jnp.mean(center * center, axis=-1, keepdims=True)
    normed = (
        center * lax.rsqrt(spread + EPS) * (1.0 + condition_ref[1:2, :]) + condition_ref[0:1, :]
    )
    left, right = normed[:, :HALF], normed[:, HALF:]
    first = core_ref[0] == 0
    keep_ref[...] = jnp.where(first, left, right).astype(jnp.bfloat16)
    send_ref[...] = jnp.where(first, right, left).astype(jnp.bfloat16)


def normalise(core, window, condition):
    return pl.pallas_call(
        norm_body,
        in_specs=[SCALARS, WHOLE, WHOLE],
        out_shape=[jax.ShapeDtypeStruct((TOK, HALF), jnp.bfloat16)] * 2,
        name="normalise",
    )(core, window, condition)


def pair_body(mine_ref, other_ref, *outs):
    for p in range(2):
        outs[p][:TOK, :] = mine_ref[:, p * PW : (p + 1) * PW]
        outs[p][TOK:, :] = other_ref[:, p * PW : (p + 1) * PW]


def pair_frames(mine, other):
    return pl.pallas_call(
        pair_body,
        out_shape=[jax.ShapeDtypeStruct((2 * TOK, PW), jnp.bfloat16)] * 2,
        name="pair_frames",
    )(mine, other)


def merge_body(held_ref, got_ref, out_ref):
    rows = held_ref.shape[0]
    out_ref[:rows, :] = held_ref[...]
    out_ref[rows:, :] = got_ref[...]


def merge(held, got):
    rows, width = held.shape
    return pl.pallas_call(
        merge_body,
        out_shape=jax.ShapeDtypeStruct((2 * rows, width), held.dtype),
        name="merge",
    )(held, got)


def block_table():
    table = []
    for core in range(2):
        rows = []
        for p in range(2):
            for j in range(32):
                rows.append(
                    sum(BIT[GATHER[step][p][core]] for step in range(5) if (j >> step) & 1)
                )
        table.append(rows)
    return table


def qkv_add(table, parts, w_ref, acc_ref, last):
    for p in range(2):
        w = jnp.concatenate([w_ref[c, p * PW : (p + 1) * PW, :] for c in range(3)], axis=1)
        product = jnp.dot(parts[p][...], w, preferred_element_type=jnp.float32)
        for j in range(16):
            block = pl.multiple_of(table[p * 32 + last * 16 + j] * TOK, TOK)
            for f in range(2):
                at = (2 * j + f) * TOK
                acc_ref[f, pl.ds(block, TOK), :] += product[at : at + TOK, :]


def qkv_first(core_ref, table, part_0, part_1, w_ref, acc_ref):
    acc_ref[...] = jnp.zeros(acc_ref.shape, jnp.float32)
    qkv_add(table, (part_0, part_1), w_ref, acc_ref, 0)


def qkv_last(core_ref, table, part_0, part_1, w_ref, before_ref, mine_ref, other_ref, acc_ref):
    acc_ref[...] = before_ref[...]
    qkv_add(table, (part_0, part_1), w_ref, acc_ref, 1)
    mine_ref[...] = acc_ref[0]
    other_ref[...] = acc_ref[1]


def qkv_sum(mine_ref, got_ref, query_ref, key_value_ref):
    total = mine_ref[...] + got_ref[...]
    query_ref[...] = total[:, :HD].astype(jnp.bfloat16)
    key_value_ref[...] = total[:, HD:].astype(jnp.bfloat16)


def qkv_call(body, name, core, table, parts, w_qkv, more, outs, scratch):
    def whole(*shape):
        return pl.BlockSpec(shape, lambda i, c, t: (0,) * len(shape))

    return pl.pallas_call(
        body,
        grid_spec=pltpu.PrefetchScalarGridSpec(
            num_scalar_prefetch=2,
            grid=(1,),
            in_specs=[whole(FT, PW)] * 2
            + [pl.BlockSpec((3, HALF, HD), lambda i, c, t: (0, c[0], 0))]
            + [whole(*m.shape) for m in more],
            out_specs=[whole(*o) for o in outs],
            scratch_shapes=scratch,
        ),
        out_shape=[jax.ShapeDtypeStruct(o, jnp.float32) for o in outs],
        cost_estimate=pl.CostEstimate(
            flops=2 * 2 * FT * HALF * 3 * HD // 2, bytes_accessed=5 << 20, transcendentals=0
        ),
        name=name,
    )(core, table, *parts, w_qkv, *more)


def project(core, held, last, w_qkv):
    tables = jnp.asarray(block_table(), jnp.int32)
    table = jnp.where(core[0] == 0, tables[0], tables[1])
    acc = (2, FT, 3 * HD)
    begun = qkv_call(qkv_first, "qkv_first", core, table, held, w_qkv, (), [acc], [])
    mine, other = qkv_call(
        qkv_last, "qkv_last", core, table, last, w_qkv, begun, [acc[1:]] * 2,
        [pltpu.VMEM(acc, jnp.float32)],
    )
    return pl.pallas_call(
        qkv_sum,
        out_shape=[
            jax.ShapeDtypeStruct((FT, HD), jnp.bfloat16),
            jax.ShapeDtypeStruct((FT, 2 * HD), jnp.bfloat16),
        ],
        name="qkv_sum",
    )(mine, other_core(other))


def attention_body(limits, q_ref, k0, v0, k1, v1, kv0, kv1, o_ref, stat_ref):
    chunks = []
    for c, (k, v) in enumerate(((k0, v0), (k1, v1))):
        for at in range(0, k.shape[0], CHUNK):
            chunks.append((k, v, 0, 0, at, min(CHUNK, k.shape[0] - at), limits[c] - at))
    for c, kv in enumerate((kv0, kv1)):
        chunks.append((kv, kv, 0, HD, 0, FT, limits[2 + c]))
    any_key = (limits[0] > 0) | (limits[1] > 0) | (limits[2] > 0) | (limits[3] > 0)
    rows = 256
    ones = jnp.ones((CHUNK, HD), jnp.bfloat16)

    def one_block(index, carry):
        start = pl.multiple_of(index * rows, rows)
        q = q_ref[pl.ds(start, rows), :]
        peak = jnp.full((rows, 1), NEG, jnp.float32)
        acc = jnp.zeros((rows, 2 * HD), jnp.float32)
        for k, v, kc, vc, at, size, limit in chunks:
            s = lax.dot_general(
                q,
                k[at : at + size, kc : kc + HD],
                (((1,), (1,)), ((), ())),
                preferred_element_type=jnp.float32,
            )
            inside = lax.broadcasted_iota(jnp.int32, (1, size), 1) < limit
            s = jnp.where(inside, s, NEG)
            newest = jnp.maximum(peak, jnp.max(s, axis=-1, keepdims=True))
            w = jnp.exp2((s - newest) * EXP_SCALE).astype(jnp.bfloat16)
            values = jnp.concatenate([v[at : at + size, vc : vc + HD], ones[:size]], axis=1)
            acc = acc * jnp.exp2((peak - newest) * EXP_SCALE) + jnp.dot(
                w, values, preferred_element_type=jnp.float32
            )
            peak = newest
        total = acc[:, HD:]
        o_ref[pl.ds(start, rows), :] = jnp.where(any_key, acc[:, :HD] / total, 0.0).astype(
            jnp.bfloat16
        )
        level = jnp.where(any_key, peak * EXP_SCALE + jnp.log2(total), NEG)
        stat_ref[pl.ds(index, 1), :] = level.T[0:1, :]
        return carry

    lax.fori_loop(0, FT // rows, one_block, 0)
    flat = jnp.concatenate([stat_ref[i : i + 1, :] for i in range(FT // rows)], axis=1)
    high = flat.astype(jnp.bfloat16).astype(jnp.float32)
    rest = flat - high
    middle = rest.astype(jnp.bfloat16).astype(jnp.float32)
    low = rest - middle
    lines = []
    for piece in (high, middle, low):
        for at in range(0, FT, HD):
            lines.append(piece[:, at : at + HD])
    lines.append(jnp.zeros((4, HD), jnp.float32))
    o_ref[FT:, :] = jnp.concatenate(lines, axis=0).astype(jnp.bfloat16)


def attention(limits, q, k0, v0, k1, v1, kv0, kv1):
    return pl.pallas_call(
        attention_body,
        in_specs=[SCALARS] + [WHOLE] * 7,
        out_shape=jax.ShapeDtypeStruct((PAY, HD), jnp.bfloat16),
        scratch_shapes=[pltpu.VMEM((8, 256), jnp.float32)],
        cost_estimate=pl.CostEstimate(
            flops=4 * FT * 5120 * HD, bytes_accessed=3 << 20, transcendentals=FT * 5120
        ),
        name="attention",
    )(limits, q, k0, v0, k1, v1, kv0, kv1)


def combine_body(*refs):
    parts, outs = refs[:4], refs[4:]
    levels = []
    for part in parts:
        lines = part[FT:, :].astype(jnp.float32)
        level = (lines[0:4] + lines[4:8]) + lines[8:12]
        row = jnp.concatenate([level[i : i + 1, :] for i in range(4)], axis=1)
        levels.append(jnp.broadcast_to(row, (HD, FT)).T)
    peak = levels[0]
    for level in levels[1:]:
        peak = jnp.maximum(peak, level)
    total = jnp.zeros((FT, HD), jnp.float32)
    acc = jnp.zeros((FT, HD), jnp.float32)
    for part, level in zip(parts, levels):
        w = jnp.exp2(level - peak)
        total = total + w
        acc = acc + w * part[:FT, :].astype(jnp.float32)
    attended = (acc / total).astype(jnp.bfloat16)
    for i in range(4):
        outs[i][...] = attended[i * ROWS : (i + 1) * ROWS, :]


def combine(parts):
    return pl.pallas_call(
        combine_body,
        out_shape=[jax.ShapeDtypeStruct((ROWS, HD), jnp.bfloat16)] * 4,
        name="combine",
    )(*parts)


def stack_body(*refs):
    for i in range(4):
        refs[4][i * ROWS : (i + 1) * ROWS, :] = refs[i][...]


def stack(blocks):
    return pl.pallas_call(
        stack_body, out_shape=jax.ShapeDtypeStruct((FT, HD), jnp.bfloat16), name="stack"
    )(*blocks)


def insert_rows(shard, fresh_rows, first, length):
    shard_rows, width = shard.shape
    frame_tokens = fresh_rows.shape[0]
    offset = jnp.clip(length - first, -frame_tokens, shard_rows)
    padding = jnp.zeros((shard_rows, width), shard.dtype)
    padded = jnp.concatenate([padding, fresh_rows, padding], 0)
    placed = lax.dynamic_slice_in_dim(padded, shard_rows - offset, shard_rows, 0)
    position = first + jnp.arange(shard_rows, dtype=jnp.int32)
    inside = (position >= length) & (position < length + frame_tokens)
    return jnp.where(inside[:, None], placed, shard)


def in_token_order(relative):
    width = relative.shape[-1]
    blocks = relative.reshape(2, 2, 2, 2, 2, TOK, width)

    def ring(blocks, axis, index):
        pieces = [
            lax.index_in_dim(lax.index_in_dim(blocks, a, axis, True), b, axis + 1, True)
            for a, b in ((0, 0), (1, 0), (1, 1), (0, 1))
        ]
        pieces = [p.reshape(p.shape[:axis] + (1,) + p.shape[axis + 2 :]) for p in pieces]
        stacked = jnp.concatenate(pieces, axis)
        low = jnp.concatenate([lax.slice_in_dim(stacked, i ^ 1, (i ^ 1) + 1, axis=axis) for i in range(4)], axis)
        stacked = jnp.where(index & 1 == 1, low, stacked)
        high = jnp.concatenate([lax.slice_in_dim(stacked, i ^ 2, (i ^ 2) + 1, axis=axis) for i in range(4)], axis)
        return jnp.where(index & 2 == 2, high, stacked)

    blocks = ring(blocks, 3, lax.axis_index("y"))
    blocks = jnp.where(lax.axis_index("zl") == 1, jnp.flip(blocks, 2), blocks)
    blocks = ring(blocks, 0, lax.axis_index("x"))
    return blocks.reshape(FT, width)


def out_body(order, t0, t1, t2, t3, other, w0, w1, w2, w3, keep_ref, send_ref, lhs_ref):
    first = order[8] == 0
    for b in range(8):
        block = pl.multiple_of(order[b] * TOK, TOK)
        here = [t[pl.ds(block, TOK), :] for t in (t0, t1, t2, t3)]
        there = [other[pl.ds(h * ROWS + block, TOK), :] for h in range(4)]
        for at, rows in ((2 * b * TOK, here), ((2 * b + 1) * TOK, there)):
            rows[1:3] = jnp.where(first, rows[1], rows[2]), jnp.where(first, rows[2], rows[1])
            lhs_ref[at : at + TOK, :] = jnp.concatenate(rows, axis=1)
    weights = jnp.concatenate([w[...] for w in (w0, w1, w2, w3)], axis=0)
    product = jnp.dot(lhs_ref[...], weights, preferred_element_type=jnp.float32)
    keep_ref[...] = product[:ROWS].astype(jnp.bfloat16)
    send_ref[...] = product[ROWS:].astype(jnp.bfloat16)


def out_project(order, tokens, other, weights):
    return pl.pallas_call(
        out_body,
        in_specs=[SCALARS] + [WHOLE] * 9,
        out_shape=[jax.ShapeDtypeStruct((ROWS, HALF), jnp.bfloat16)] * 2,
        scratch_shapes=[pltpu.VMEM((2 * ROWS, 4 * HD), jnp.bfloat16)],
        name="out_project",
    )(order, *tokens, other, *weights)


def add_body(keep_ref, got_ref, *outs):
    total = keep_ref[...].astype(jnp.float32) + got_ref[...].astype(jnp.float32)
    rows = total.shape[0] // 2
    for i in range(2):
        outs[i][...] = total[i * rows : (i + 1) * rows].astype(outs[i].dtype)


def add_up(keep, got, dtype):
    rows, width = keep.shape
    return pl.pallas_call(
        add_body,
        out_shape=[jax.ShapeDtypeStruct((rows // 2, width), dtype)] * 2,
        name="add_up",
    )(keep, got)


def finish_body(core_ref, mine_ref, got_ref, window_ref, gate_ref, out_ref):
    first = core_ref[0] == 0
    mine, got = mine_ref[...], got_ref[...]
    for i in range(2):
        columns = slice(i * HALF, (i + 1) * HALF)
        product = jnp.where(first, mine, got) if i == 0 else jnp.where(first, got, mine)
        base = window_ref[0, :, columns].astype(jnp.float32)
        out_ref[:, columns] = (base + gate_ref[2:3, columns] * product).astype(jnp.bfloat16)


def finish(core, mine, got, window, condition):
    return pl.pallas_call(
        finish_body,
        in_specs=[SCALARS] + [WHOLE] * 4,
        out_shape=jax.ShapeDtypeStruct((TOK, D), jnp.bfloat16),
        name="finish",
    )(core, mine, got, window, condition)


def on_device(
    window,
    levels,
    actions,
    cache_len,
    level_table,
    action_table,
    w_qkv,
    w_out,
    cache_keys,
    cache_values,
    fresh_frame,
):
    core = lax.axis_index("core")
    cores = core.astype(jnp.int32).reshape(1)
    zh = lax.axis_index("zh")
    slot = lax.axis_index(FRAME)
    length = cache_len[0]
    shard_rows = cache_keys.shape[0]

    condition = (
        lax.dynamic_slice_in_dim(level_table, levels[0], 1, 0)
        + lax.dynamic_slice_in_dim(action_table, actions[0], 1, 0)
    )[0]
    keep, send = normalise(cores, window, condition)

    held = list(pair_frames(keep, other_core(send)))
    for step in range(4):
        got = [across(held[p], GATHER[step][p]) for p in range(2)]
        held = [merge(held[p], got[p]) for p in range(2)]
        if step == 1:
            late_keys, late_values, *held = lax.optimization_barrier(
                (cache_keys, cache_values, *held)
            )
    last = [across(held[p], GATHER[4][p]) for p in range(2)]

    other_keys, other_values, *last = lax.optimization_barrier(
        (other_core(late_keys), other_core(late_values), *last)
    )

    query, key_value = project(cores, held, last, w_qkv)

    q_up = frame_shift(query, -2)
    q_down = frame_shift(query, 2)
    other_key_value = other_core(key_value)

    w_own = lax.dynamic_slice_in_dim(after(w_out, query), core * HALF, HALF, 1)
    w_first = across(w_own, SPREAD[0])
    w_second = across(w_own, SPREAD[1])

    def attend(q, ahead):
        frame = (slot + ahead) % 8
        partner = slot ^ 1
        limits = jnp.stack(
            [
                length - slot * shard_rows,
                length - partner * shard_rows,
                jnp.where(slot <= frame, FT, 0),
                jnp.where(partner <= frame, FT, 0),
            ]
        ).astype(jnp.int32)
        return attention(
            limits, q, cache_keys, cache_values, other_keys, other_values, key_value, other_key_value
        )

    part = attend(query, 0)
    sent = [part]
    part, q_up, q_down = lax.optimization_barrier((part, q_up, q_down))
    q_far = [frame_shift(q_up[: FT // 2], -2), frame_shift(q_down[FT // 2 :], 2)]
    part = attend(q_up, 2)
    sent.append(frame_shift(part, 2))
    part, q_down, w_first = lax.optimization_barrier((part, q_down, w_first))
    w_both = across(w_first, SPREAD[1])
    part = attend(q_down, 6)
    sent.append(frame_shift(part, -2))
    part, q_far = lax.optimization_barrier((part, q_far))
    part = attend(jnp.concatenate(q_far, 0), 4)
    sent.append(frame_shift(part, 4))
    root = in_token_order(after(key_value, part))

    blocks = combine(sent)
    tokens = [
        blocks[0],
        across(blocks[2], (XA, XA)),
        across(blocks[1], (XB, XB)),
        lax.ppermute(blocks[3], "x", [(i, i ^ 2) for i in range(4)]),
    ]
    order = jnp.where(
        core == 0,
        jnp.array([*range(8), 0], jnp.int32),
        jnp.array([(b & 1) * 4 + (b >> 1) for b in range(8)] + [1], jnp.int32),
    )
    keep, send = out_project(
        order, tokens, other_core(stack(tokens)), [w_own, w_first, w_second, w_both]
    )
    got = across(send, REDUCE[0])
    root_far = lax.ppermute(after(root, send), FRAME, [(0, 4)])
    keep, send = add_up(keep, got, jnp.bfloat16)
    got = across(send, REDUCE[1])
    root, _ = lax.optimization_barrier((jnp.where(zh == 2, root_far, root), send))
    root_odd = lax.ppermute(root, FRAME, [(0, 2), (4, 6)])
    keep, send = add_up(keep, got, jnp.bfloat16)
    got = across(send, REDUCE[2])
    root, _ = lax.optimization_barrier((jnp.where(zh % 2 == 1, root_odd, root), send))
    root = jnp.where(core == 1, lax.ppermute(root, "core", [(0, 1)]), root)
    first_row = slot * shard_rows
    new_keys = insert_rows(cache_keys, root[:, :HD], first_row, length)
    new_values = insert_rows(cache_values, root[:, HD:], first_row, length)
    total = add_up(keep, got, jnp.float32)
    updated = finish(cores, total[0], other_core(total[1]), window, condition)

    moved = frame_shift(updated, -1)
    next_window = jnp.where(slot == 7, fresh_frame, moved)
    arrived = [lax.ppermute(updated, FRAME, [(0, 2 * d)]) for d in (2, 1, 3)]
    finished = jnp.where(slot == 0, updated, arrived[0] + arrived[1] + arrived[2])
    finished = jnp.where(core == 1, lax.ppermute(finished, "core", [(0, 1)]), finished)
    return (next_window[None], finished, new_keys, new_values)


def solution(mesh):
    split = Mesh(mesh.devices.reshape(4, 2, 4, 2, 4), FRAME + FSDP)
    return jax.shard_map(
        on_device,
        mesh=split,
        in_specs=(
            P(FRAME, FSDP, None),
            P(FRAME),
            P(FRAME),
            P(),
            P(),
            P(),
            P(None, None, FSDP),
            P(FSDP, None),
            P(FRAME, FSDP),
            P(FRAME, FSDP),
            P(FSDP, None),
        ),
        out_specs=(P(FRAME, FSDP, None), P(FSDP, None), P(FRAME, FSDP), P(FRAME, FSDP)),
        check_vma=False,
    )
```

```python
import math

import jax
import jax.numpy as jnp
from jax import lax
from jax.experimental import pallas as pl
from jax.experimental.pallas import tpu as pltpu
from jax.sharding import Mesh
from jax.sharding import PartitionSpec as P

HD = 128
D = 5120
FT = 512
TOK = 16
ROWS = FT // 4
HALF = D // 2
EPS = 1e-06
NEG = -1e30
LOG2E = math.log2(math.e)
EXP_SCALE = LOG2E / math.sqrt(HD)
CHUNK = 1024
PAY = FT + 16

FRAME = ("zh", "core")
FSDP = ("x", "zl", "y")

ROOM = pltpu.CompilerParams(vmem_limit_bytes=28 << 20)


DIMS = (("x", 1, 4), ("x", 3, 4), ("zl", 1, 2), ("y", 1, 4), ("y", 3, 4))


def held_near(*blocks):
    return [pltpu.with_memory_space_constraint(b, pltpu.VMEM) for b in blocks]


def across(block, dim):
    axis, mask, size = DIMS[dim]
    return lax.ppermute(block, axis, [(i, i ^ mask) for i in range(size)])


def frame_shift(block, distance):
    return lax.ppermute(block, FRAME, [(i, (i + distance) % 8) for i in range(8)])


def other_core(block):
    return lax.ppermute(block, "core", [(0, 1), (1, 0)])


def pieces_of(value):
    high = value.astype(jnp.bfloat16).astype(jnp.float32)
    rest = value - high
    middle = rest.astype(jnp.bfloat16).astype(jnp.float32)
    return high, middle, rest - middle


def norm_body(window_ref, condition_ref, out_ref, carry_ref):
    rows = window_ref[0].astype(jnp.float32)
    center = rows - jnp.mean(rows, axis=-1, keepdims=True)
    spread = jnp.mean(center * center, axis=-1, keepdims=True)
    out_ref[...] = (
        center * lax.rsqrt(spread + EPS) * (1.0 + condition_ref[1:2, :]) + condition_ref[0:1, :]
    ).astype(jnp.bfloat16)
    carry_ref[:TOK, :] = window_ref[0]
    gate = pieces_of(condition_ref[2:3, :])
    empty = jnp.zeros((TOK - 3, D), jnp.float32)
    carry_ref[TOK:, :] = jnp.concatenate([*gate, empty], axis=0).astype(jnp.bfloat16)


def normalise(window, condition):
    return pl.pallas_call(
        norm_body,
        out_shape=[
            pltpu.VMEM((TOK, D), jnp.bfloat16),
            pltpu.VMEM((2 * TOK, D), jnp.bfloat16),
        ],
        compiler_params=ROOM,
        name="normalise",
    )(window, condition)


def halves_body(*refs):
    blocks, outs = refs[:-2], refs[-2:]
    for i, block in enumerate(blocks):
        for h in range(2):
            outs[h][i * TOK : (i + 1) * TOK, :] = block[:, h * HALF : (h + 1) * HALF]


def halves(mine, got):
    return pl.pallas_call(
        halves_body,
        out_shape=[pltpu.VMEM((2 * TOK, HALF), jnp.bfloat16)] * 2,
        compiler_params=ROOM,
        name="halves",
    )(*held_near(mine, got))


def join_body(*refs):
    rows = refs[0].shape[0]
    for h in range(2):
        for i in range(4):
            refs[8 + h][i * rows : (i + 1) * rows, :] = refs[4 * h + i][...]


def join(first, second):
    shape = pltpu.VMEM((4 * first[0].shape[0], HALF), jnp.bfloat16)
    return pl.pallas_call(
        join_body, out_shape=[shape] * 2, compiler_params=ROOM, name="join"
    )(*held_near(*first, *second))


def after(block, *earlier):
    return lax.optimization_barrier((block, *earlier))[0]


def ring(block, axis, core):
    before = lax.ppermute(block, axis, [(i, (i + 1) % 4) for i in range(4)])
    behind = lax.ppermute(block, axis, [(i, (i - 1) % 4) for i in range(4)])
    pairs = [
        (c * 4 + i, c * 4 + (i + (1, -1)[c]) % 4) for c in range(2) for i in range(4)
    ]
    opposite = lax.ppermute(jnp.where(core == 0, before, behind), ("core", axis), pairs)
    return before, behind, opposite


def qkv_body(count, last, table, *refs):
    blocks, w_ref, refs = refs[: 2 * count], refs[2 * count], refs[2 * count + 1 :]
    if last:
        before_ref, query_ref, key_value_ref, acc_ref = refs
    elif len(refs) == 2:
        before_ref, acc_ref = refs
    else:
        before_ref, acc_ref = None, refs[0]
    if before_ref is None:
        acc_ref[...] = jnp.zeros(acc_ref.shape, jnp.float32)
    else:
        acc_ref[...] = before_ref[...]
    for h in range(2):
        w = jnp.concatenate(
            [w_ref[c, h * HALF : (h + 1) * HALF, :] for c in range(3)], axis=1
        )
        for i in range(count):
            product = jnp.dot(blocks[2 * i + h][...], w, preferred_element_type=jnp.float32)
            for j in range(8):
                at = pl.multiple_of(table[(h * count + i) * 8 + j] * TOK, TOK)
                acc_ref[pl.ds(at, TOK), :] += product[j * TOK : (j + 1) * TOK, :]
    if last:
        query_ref[...] = acc_ref[:, :HD].astype(jnp.bfloat16)
        key_value_ref[...] = acc_ref[:, HD:].astype(jnp.bfloat16)


def qkv_add(table, pairs, w_qkv, before, last):
    count = len(pairs)
    acc = pltpu.VMEM((FT, 3 * HD), jnp.float32)
    operands = held_near(*[b for pair in pairs for b in pair])
    operands += [w_qkv] + ([] if before is None else held_near(before))
    outs = [
        pltpu.VMEM((FT, HD), jnp.bfloat16),
        pltpu.VMEM((FT, 2 * HD), jnp.bfloat16),
    ]
    return pl.pallas_call(
        lambda *refs: qkv_body(count, last, *refs),
        in_specs=[pl.BlockSpec(memory_space=pltpu.SMEM)]
        + [pl.BlockSpec(memory_space=pltpu.VMEM)] * len(operands),
        out_shape=outs if last else acc,
        scratch_shapes=[pltpu.VMEM(acc.shape, jnp.float32)] if last else [],
        cost_estimate=pl.CostEstimate(
            flops=2 * count * ROWS * D * 3 * HD, bytes_accessed=6 << 20, transcendentals=0
        ),
        compiler_params=ROOM,
        name="qkv_last" if last else "qkv_add",
    )(table, *operands)


def places(pieces):
    odd = {"x": lax.axis_index("x") % 2 == 1, "y": lax.axis_index("y") % 2 == 1}
    bits = {"x": (16, 8), "y": (2, 1)}

    def place(axis, piece):
        one, three = bits[axis]
        if piece == 0:
            return 0
        if piece == 3:
            return one + three
        return jnp.where(odd[axis] == (piece == 1), one, three)

    table = []
    for near, far in (("x", "y"), ("y", "x")):
        for piece in pieces:
            for j in range(8):
                table.append(place(far, piece) + place(near, j // 2) + 4 * (j % 2))
    return jnp.stack([jnp.asarray(t, jnp.int32) for t in table])


def attention_body(limits, q_ref, k0, v0, k1, v1, kv0, kv1, o_ref, stat_ref):
    chunks = []
    for c, (k, v) in enumerate(((k0, v0), (k1, v1))):
        for at in range(0, k.shape[0], CHUNK):
            chunks.append((k, v, 0, 0, at, min(CHUNK, k.shape[0] - at), limits[c] - at))
    for c, kv in enumerate((kv0, kv1)):
        chunks.append((kv, kv, 0, HD, 0, FT, limits[2 + c]))
    any_key = (limits[0] > 0) | (limits[1] > 0) | (limits[2] > 0) | (limits[3] > 0)
    rows = 256
    ones = jnp.ones((CHUNK, HD), jnp.bfloat16)

    def one_block(index, carry):
        start = pl.multiple_of(index * rows, rows)
        q = q_ref[pl.ds(start, rows), :]
        peak = jnp.full((rows, 1), NEG, jnp.float32)
        acc = jnp.zeros((rows, 2 * HD), jnp.float32)
        for k, v, kc, vc, at, size, limit in chunks:
            s = lax.dot_general(
                q,
                k[at : at + size, kc : kc + HD],
                (((1,), (1,)), ((), ())),
                preferred_element_type=jnp.float32,
            )
            inside = lax.broadcasted_iota(jnp.int32, (1, size), 1) < limit
            s = jnp.where(inside, s, NEG)
            newest = jnp.maximum(peak, jnp.max(s, axis=-1, keepdims=True))
            w = jnp.exp2((s - newest) * EXP_SCALE).astype(jnp.bfloat16)
            values = jnp.concatenate([v[at : at + size, vc : vc + HD], ones[:size]], axis=1)
            acc = acc * jnp.exp2((peak - newest) * EXP_SCALE) + jnp.dot(
                w, values, preferred_element_type=jnp.float32
            )
            peak = newest
        total = acc[:, HD:]
        o_ref[pl.ds(start, rows), :] = jnp.where(any_key, acc[:, :HD] / total, 0.0).astype(
            jnp.bfloat16
        )
        level = jnp.where(any_key, peak * EXP_SCALE + jnp.log2(total), NEG)
        stat_ref[pl.ds(index, 1), :] = level.T[0:1, :]
        return carry

    lax.fori_loop(0, FT // rows, one_block, 0)
    flat = jnp.concatenate([stat_ref[i : i + 1, :] for i in range(FT // rows)], axis=1)
    lines = []
    for piece in pieces_of(flat):
        for at in range(0, FT, HD):
            lines.append(piece[:, at : at + HD])
    lines.append(jnp.zeros((4, HD), jnp.float32))
    o_ref[FT:, :] = jnp.concatenate(lines, axis=0).astype(jnp.bfloat16)


def attention(limits, q, k0, v0, k1, v1, kv0, kv1):
    whole = pl.BlockSpec(memory_space=pltpu.VMEM)
    return pl.pallas_call(
        attention_body,
        in_specs=[pl.BlockSpec(memory_space=pltpu.SMEM)] + [whole] * 7,
        out_shape=pltpu.VMEM((PAY, HD), jnp.bfloat16),
        scratch_shapes=[pltpu.VMEM((8, 256), jnp.float32)],
        cost_estimate=pl.CostEstimate(
            flops=4 * FT * 5120 * HD, bytes_accessed=3 << 20, transcendentals=FT * 5120
        ),
        compiler_params=ROOM,
        name="attention",
    )(limits, q, k0, v0, k1, v1, kv0, kv1)


def combine_body(*refs):
    parts, o_ref = refs[:-1], refs[-1]
    levels = []
    for part in parts:
        lines = part[FT:, :].astype(jnp.float32)
        level = (lines[0:4] + lines[4:8]) + lines[8:12]
        row = jnp.concatenate([level[i : i + 1, :] for i in range(4)], axis=1)
        levels.append(jnp.broadcast_to(row, (HD, FT)).T)
    peak = levels[0]
    for level in levels[1:]:
        peak = jnp.maximum(peak, level)
    total = jnp.zeros((FT, HD), jnp.float32)
    acc = jnp.zeros((FT, HD), jnp.float32)
    for part, level in zip(parts, levels):
        w = jnp.exp2(level - peak)
        total = total + w
        acc = acc + w * part[:FT, :].astype(jnp.float32)
    o_ref[...] = (acc / total).astype(jnp.bfloat16)


def combine(parts):
    return pl.pallas_call(
        combine_body,
        out_shape=pltpu.VMEM((FT, HD), jnp.bfloat16),
        compiler_params=ROOM,
        name="combine",
    )(*held_near(*parts))


def insert_rows(shard, fresh_rows, first, length):
    shard_rows, width = shard.shape
    frame_tokens = fresh_rows.shape[0]
    offset = jnp.clip(length - first, -frame_tokens, shard_rows)
    padding = jnp.zeros((shard_rows, width), shard.dtype)
    padded = jnp.concatenate([padding, fresh_rows, padding], 0)
    placed = lax.dynamic_slice_in_dim(padded, shard_rows - offset, shard_rows, 0)
    position = first + jnp.arange(shard_rows, dtype=jnp.int32)
    inside = (position >= length) & (position < length + frame_tokens)
    return jnp.where(inside[:, None], placed, shard)


def in_token_order(relative):
    width = relative.shape[-1]
    blocks = relative.reshape(2, 2, 2, 2, 2, TOK, width)

    def ring(blocks, axis, index):
        pieces = [
            lax.index_in_dim(lax.index_in_dim(blocks, a, axis, True), b, axis + 1, True)
            for a, b in ((0, 0), (1, 0), (1, 1), (0, 1))
        ]
        pieces = [p.reshape(p.shape[:axis] + (1,) + p.shape[axis + 2 :]) for p in pieces]
        stacked = jnp.concatenate(pieces, axis)
        low = jnp.concatenate([lax.slice_in_dim(stacked, i ^ 1, (i ^ 1) + 1, axis=axis) for i in range(4)], axis)
        stacked = jnp.where(index & 1 == 1, low, stacked)
        high = jnp.concatenate([lax.slice_in_dim(stacked, i ^ 2, (i ^ 2) + 1, axis=axis) for i in range(4)], axis)
        return jnp.where(index & 2 == 2, high, stacked)

    blocks = ring(blocks, 3, lax.axis_index("y"))
    blocks = jnp.where(lax.axis_index("zl") == 1, jnp.flip(blocks, 2), blocks)
    blocks = ring(blocks, 0, lax.axis_index("x"))
    return blocks.reshape(FT, width)


CUTS = (0, 1792, 3456, 5120)
RING = (2, 3, 4)
QUARTER = D // 4


def split_rows(axis, bit):
    return [r * TOK for r in range(8) if (r >> (2 - axis)) & 1 == bit]


def out_body(*refs):
    tokens = jnp.concatenate([r[...] for r in refs[:4]], axis=1)
    quarters, keeps, sends, y_ref = refs[4:20], refs[20:23], refs[23:26], refs[26]
    for c in range(4):
        weights = jnp.concatenate([w[...] for w in quarters[4 * c : 4 * c + 4]], axis=0)
        y_ref[:, c * QUARTER : (c + 1) * QUARTER] = jnp.dot(
            tokens, weights, preferred_element_type=jnp.float32
        ).astype(jnp.bfloat16)
    for p in range(3):
        for bit, out in ((0, keeps[p]), (1, sends[p])):
            for i, r in enumerate(split_rows(p, bit)):
                out[i * TOK : (i + 1) * TOK, :] = y_ref[r : r + TOK, CUTS[p] : CUTS[p + 1]]


def out_project(tokens, quarters):
    widths = [CUTS[p + 1] - CUTS[p] for p in range(3)]
    shapes = [pltpu.VMEM((ROWS // 2, w), jnp.bfloat16) for w in widths]
    outs = pl.pallas_call(
        out_body,
        out_shape=shapes + shapes,
        scratch_shapes=[pltpu.VMEM((ROWS, D), jnp.bfloat16)],
        compiler_params=ROOM,
        name="out_project",
    )(*held_near(*tokens), *quarters)
    return outs[:3], outs[3:]


def add_body(*refs):
    keeps, gots, next_keeps, next_sends = refs[:3], refs[3:6], refs[6:9], refs[9:]
    for p in range(3):
        total = keeps[p][...].astype(jnp.float32) + gots[p][...].astype(jnp.float32)
        total = total.astype(jnp.bfloat16)
        left = [d for d in (0, 1, 2) if d != p] if total.shape[0] == 4 * TOK else []
        if left:
            axis = left.index((p + 1) % 3)
            blocks = [[r for r in range(4) if (r >> (1 - axis)) & 1 == bit] for bit in (0, 1)]
        else:
            blocks = [[0], [1]]
        for ids, out in zip(blocks, (next_keeps[p], next_sends[p])):
            for i, r in enumerate(ids):
                out[i * TOK : (i + 1) * TOK, :] = total[r * TOK : (r + 1) * TOK, :]


def add_up(keeps, gots):
    rows = keeps[0].shape[0] // 2
    shapes = [pltpu.VMEM((rows, k.shape[1]), jnp.bfloat16) for k in keeps] * 2
    outs = pl.pallas_call(add_body, out_shape=shapes, compiler_params=ROOM, name="add_up")(*held_near(*keeps, *gots))
    return outs[:3], outs[3:]


def finish_body(core_ref, *refs):
    keeps, gots, carry_ref, out_ref = refs[:3], refs[3:6], refs[6], refs[7]
    total = jnp.concatenate(
        [k[...].astype(jnp.float32) + g[...].astype(jnp.float32) for k, g in zip(keeps, gots)], 1
    )
    near, far = total[:, :HALF], total[:, HALF:]
    lines = carry_ref[TOK:, :].astype(jnp.float32)
    gate = (lines[0:1] + lines[1:2]) + lines[2:3]
    base = carry_ref[:TOK, :].astype(jnp.float32)
    first = core_ref[0] == 0
    for h, product in ((0, jnp.where(first, near, far)), (1, jnp.where(first, far, near))):
        columns = slice(h * HALF, (h + 1) * HALF)
        out_ref[:, columns] = (base[:, columns] + gate[:, columns] * product).astype(jnp.bfloat16)


def finish(core, keeps, gots, carry):
    return pl.pallas_call(
        finish_body,
        in_specs=[pl.BlockSpec(memory_space=pltpu.SMEM)]
        + [pl.BlockSpec(memory_space=pltpu.VMEM)] * 7,
        out_shape=pltpu.VMEM((TOK, D), jnp.bfloat16),
        compiler_params=ROOM,
        name="finish",
    )(core, *held_near(*keeps, *gots, carry))


def on_device(
    window,
    levels,
    actions,
    cache_len,
    level_table,
    action_table,
    w_qkv,
    w_out,
    cache_keys,
    cache_values,
    fresh_frame,
):
    core = lax.axis_index("core")
    slot = lax.axis_index(FRAME)
    length = cache_len[0]
    shard_rows = cache_keys.shape[0]

    condition = (
        lax.dynamic_slice_in_dim(level_table, levels[0], 1, 0)
        + lax.dynamic_slice_in_dim(action_table, actions[0], 1, 0)
    )[0]
    normed, carry = normalise(window, condition)

    first, second = halves(normed, across(normed, 2))
    first, second = join((first, *ring(first, "x", core)), (second, *ring(second, "y", core)))
    tables = [places(p) for p in ((0,), (1, 2), (3,))]

    late = lax.optimization_barrier((first, second, cache_keys, cache_values, carry))
    first, second = late[:2]
    other_keys = other_core(late[2])
    other_values = other_core(late[3])
    carry_next = frame_shift(late[4], -1)

    around = list(zip(ring(first, "y", core), ring(second, "x", core)))
    acc = qkv_add(tables[0], [(first, second)], w_qkv, None, False)
    acc = qkv_add(tables[1], around[:2], w_qkv, acc, False)
    acc, opposite, other_keys, other_values, carry_next = lax.optimization_barrier(
        (acc, around[2], other_keys, other_values, carry_next)
    )
    query, key_value = qkv_add(tables[2], [opposite], w_qkv, acc, True)

    q_up = frame_shift(query, -2)
    q_down = frame_shift(query, 2)
    q_far = frame_shift(query, 4)
    other_key_value = other_core(key_value)

    w_late = after(w_out, query)
    own = [lax.dynamic_slice_in_dim(w_late, core * HALF + i * QUARTER, QUARTER, 1) for i in (0, 1)]
    own += [
        lax.dynamic_slice_in_dim(w_late, (1 - core) * HALF + i * QUARTER, QUARTER, 1) for i in (0, 1)
    ]
    a_1, a_3 = across(own[0], 0), across(own[0], 1)
    b_3, b_1 = across(own[1], 1), across(own[1], 0)

    def attend(q, ahead):
        frame = (slot + ahead) % 8
        partner = slot ^ 1
        limits = jnp.stack(
            [
                length - slot * shard_rows,
                length - partner * shard_rows,
                jnp.where(slot <= frame, FT, 0),
                jnp.where(partner <= frame, FT, 0),
            ]
        ).astype(jnp.int32)
        return attention(
            limits, q, cache_keys, cache_values, other_keys, other_values, key_value, other_key_value
        )

    def from_first(block, chip):
        return lax.ppermute(block, FRAME, [(0, 2 * chip)])

    part = attend(query, 0)
    part, q_up, q_down = lax.optimization_barrier((part, q_up, q_down))
    sent = [frame_shift(part, -1)]
    root = [key_value, from_first(after(key_value, part), 2)]
    part = attend(q_up, 2)
    sent.append(frame_shift(part, 1))
    part, q_down, a_1, a_3, b_1, b_3 = lax.optimization_barrier((part, q_down, a_1, a_3, b_1, b_3))
    a_2, b_2 = across(a_1, 1), across(b_3, 0)
    part = attend(q_down, 6)
    sent.append(frame_shift(part, -3))
    part, q_far, a_2, b_2 = lax.optimization_barrier((part, q_far, a_2, b_2))
    root.append(from_first(after(key_value, part), 1))
    root.append(from_first(after(key_value, part), 3))
    near = [[own[0], a_1, a_3, a_2], [own[1], b_1, b_3, b_2]]
    far = [[own[2 + i]] + [other_core(w) for w in near[i][1:]] for i in range(2)]
    part = attend(q_far, 4)
    sent.append(frame_shift(part, 3))

    attended = combine(sent).reshape(2, 2, ROWS, HD)

    beyond = lax.ppermute(attended[1, 1], "x", [(i, i ^ 2) for i in range(4)])
    together = [attended[0, 0], across(attended[1, 0], 0), across(attended[0, 1], 1), beyond]
    keeps, sends = out_project(together, near[0] + near[1] + far[0] + far[1])
    gots = [across(sends[p], RING[p]) for p in range(3)]
    root = lax.optimization_barrier((*root, sends[0]))
    root = jnp.where(slot == 0, root[0], root[1] + root[2] + root[3])
    gots, root = lax.optimization_barrier((gots, root))
    root_beside = lax.ppermute(root, "core", [(0, 1)])
    keeps, sends = add_up(keeps, gots)
    gots = [across(sends[p], RING[(p + 1) % 3]) for p in range(3)]
    root = in_token_order(jnp.where(core == 1, root_beside, root))
    gots, root = lax.optimization_barrier((gots, root))
    keeps, sends = add_up(keeps, gots)
    gots = [across(sends[p], RING[(p + 2) % 3]) for p in range(3)]
    updated = finish(core.astype(jnp.int32).reshape(1), keeps, gots, carry_next)

    next_window = jnp.where(slot == 7, fresh_frame, updated)
    arrived = [lax.ppermute(updated, FRAME, [(7, 2 * chip + 1)]) for chip in (1, 0, 2)]
    first_row = slot * shard_rows
    root = after(root, updated)
    new_keys = insert_rows(cache_keys, root[:, :HD], first_row, length)
    new_values = insert_rows(cache_values, root[:, HD:], first_row, length)
    arrived, new_keys, new_values = lax.optimization_barrier((arrived, new_keys, new_values))
    finished = jnp.where(slot == 7, updated, arrived[0] + arrived[1] + arrived[2])
    finished = jnp.where(core == 0, lax.ppermute(finished, "core", [(1, 0)]), finished)
    return (next_window[None], finished, new_keys, new_values)


def solution(mesh):
    split = Mesh(mesh.devices.reshape(4, 2, 4, 2, 4), FRAME + FSDP)
    return jax.shard_map(
        on_device,
        mesh=split,
        in_specs=(
            P(FRAME, FSDP, None),
            P(FRAME),
            P(FRAME),
            P(),
            P(),
            P(),
            P(None, None, FSDP),
            P(FSDP, None),
            P(FRAME, FSDP),
            P(FRAME, FSDP),
            P(FSDP, None),
        ),
        out_specs=(P(FRAME, FSDP, None), P(FSDP, None), P(FRAME, FSDP), P(FRAME, FSDP)),
        check_vma=False,
    )
```

```python
import math

import jax
import jax.numpy as jnp
from jax import lax
from jax.experimental import pallas as pl
from jax.experimental.pallas import tpu as pltpu
from jax.sharding import Mesh
from jax.sharding import PartitionSpec as P

HD = 128
D = 5120
FT = 512
TOK = 16
ROWS = FT // 4
HALF = D // 2
EPS = 1e-06
NEG = -1e30
LOG2E = math.log2(math.e)
EXP_SCALE = LOG2E / math.sqrt(HD)
CHUNK = 1024
PAY = FT + 16

FRAME = ("zh", "core")
FSDP = ("x", "zl", "y")

ROOM = pltpu.CompilerParams(vmem_limit_bytes=18 << 20)


DIMS = (("x", 1, 4), ("x", 3, 4), ("zl", 1, 2), ("y", 1, 4), ("y", 3, 4))


def held_near(*blocks):
    return [pltpu.with_memory_space_constraint(b, pltpu.VMEM) for b in blocks]


def across(block, dim):
    axis, mask, size = DIMS[dim]
    return lax.ppermute(block, axis, [(i, i ^ mask) for i in range(size)])


def across_each(block, by_core):
    pairs = []
    for core in range(2):
        axis, mask, _ = DIMS[by_core[core]]
        for x in range(4):
            for zl in range(2):
                for y in range(4):
                    at = {"x": x, "zl": zl, "y": y}
                    to = dict(at, **{axis: at[axis] ^ mask})
                    pairs.append(
                        tuple(((core * 4 + p["x"]) * 2 + p["zl"]) * 4 + p["y"] for p in (at, to))
                    )
    return lax.ppermute(block, ("core", "x", "zl", "y"), pairs)


def frame_shift(block, distance):
    return lax.ppermute(block, FRAME, [(i, (i + distance) % 8) for i in range(8)])


def other_core(block):
    return lax.ppermute(block, "core", [(0, 1), (1, 0)])


def pieces_of(value):
    high = value.astype(jnp.bfloat16).astype(jnp.float32)
    rest = value - high
    middle = rest.astype(jnp.bfloat16).astype(jnp.float32)
    return high, middle, rest - middle


def norm_body(window_ref, condition_ref, out_ref, carry_ref):
    rows = window_ref[0].astype(jnp.float32)
    center = rows - jnp.mean(rows, axis=-1, keepdims=True)
    spread = jnp.mean(center * center, axis=-1, keepdims=True)
    out_ref[...] = (
        center * lax.rsqrt(spread + EPS) * (1.0 + condition_ref[1:2, :]) + condition_ref[0:1, :]
    ).astype(jnp.bfloat16)
    carry_ref[:TOK, :] = window_ref[0]
    gate = pieces_of(condition_ref[2:3, :])
    empty = jnp.zeros((TOK - 3, D), jnp.float32)
    carry_ref[TOK:, :] = jnp.concatenate([*gate, empty], axis=0).astype(jnp.bfloat16)


def normalise(window, condition):
    return pl.pallas_call(
        norm_body,
        out_shape=[
            pltpu.VMEM((TOK, D), jnp.bfloat16),
            pltpu.VMEM((2 * TOK, D), jnp.bfloat16),
        ],
        compiler_params=ROOM,
        name="normalise",
    )(window, condition)


def halves_body(*refs):
    blocks, outs = refs[:-2], refs[-2:]
    for i, block in enumerate(blocks):
        for h in range(2):
            outs[h][i * TOK : (i + 1) * TOK, :] = block[:, h * HALF : (h + 1) * HALF]


def halves(mine, got):
    return pl.pallas_call(
        halves_body,
        out_shape=[pltpu.VMEM((2 * TOK, HALF), jnp.bfloat16)] * 2,
        compiler_params=ROOM,
        name="halves",
    )(*held_near(mine, got))


def join_body(*refs):
    rows = refs[0].shape[0]
    for h in range(2):
        for i in range(4):
            refs[8 + h][i * rows : (i + 1) * rows, :] = refs[4 * h + i][...]


def join(first, second):
    shape = pltpu.VMEM((4 * first[0].shape[0], HALF), jnp.bfloat16)
    return pl.pallas_call(
        join_body, out_shape=[shape] * 2, compiler_params=ROOM, name="join"
    )(*held_near(*first, *second))


def after(block, *earlier):
    return lax.optimization_barrier((block, *earlier))[0]


def pick_body(core_ref, first_ref, second_ref, out_ref):
    @pl.when(core_ref[0] == 0)
    def _():
        out_ref[...] = first_ref[...]

    @pl.when(core_ref[0] != 0)
    def _():
        out_ref[...] = second_ref[...]


def pick(core, first, second):
    return pl.pallas_call(
        pick_body,
        in_specs=[pl.BlockSpec(memory_space=pltpu.SMEM)]
        + [pl.BlockSpec(memory_space=pltpu.VMEM)] * 2,
        out_shape=pltpu.VMEM(first.shape, first.dtype),
        compiler_params=ROOM,
        name="pick",
    )(core, *held_near(first, second))


def by_core(block, axis, routes):
    pairs = [(c * 4 + i, c * 4 + routes[c](i)) for c in range(2) for i in range(4)]
    return lax.ppermute(block, ("core", axis), pairs)


def ring(block, axis, core):
    before = lax.ppermute(block, axis, [(i, (i + 1) % 4) for i in range(4)])
    behind = lax.ppermute(block, axis, [(i, (i - 1) % 4) for i in range(4)])
    opposite = by_core(
        pick(core, before, behind), axis, (lambda i: (i + 1) % 4, lambda i: (i - 1) % 4)
    )
    return before, behind, opposite


def qkv_body(count, last, table, *refs):
    blocks, w_ref, refs, x_ref = refs[: 2 * count], refs[2 * count], refs[2 * count + 1 : -1], refs[-1]
    if last:
        before_ref, query_ref, key_value_ref, acc_ref = refs
    elif len(refs) == 2:
        before_ref, acc_ref = refs
    else:
        before_ref, acc_ref = None, refs[0]
    if before_ref is None:
        acc_ref[...] = jnp.zeros(acc_ref.shape, jnp.float32)
    else:
        acc_ref[...] = before_ref[...]
    for i in range(2 * count):
        x_ref[i] = blocks[i][...]

    def one(i, carry):
        at = pl.multiple_of((i % 2) * HALF, HALF)
        w = jnp.concatenate([w_ref[c, pl.ds(at, HALF), :] for c in range(3)], axis=1)
        product = jnp.dot(x_ref[i], w, preferred_element_type=jnp.float32)
        for j in range(8):
            at = pl.multiple_of(table[i * 8 + j] * TOK, TOK)
            acc_ref[pl.ds(at, TOK), :] += product[j * TOK : (j + 1) * TOK, :]
        return carry

    lax.fori_loop(0, 2 * count, one, 0)
    if last:
        query_ref[...] = acc_ref[:, :HD].astype(jnp.bfloat16)
        key_value_ref[...] = acc_ref[:, HD:].astype(jnp.bfloat16)


def qkv_add(table, pairs, w_qkv, before, last):
    count = len(pairs)
    acc = pltpu.VMEM((FT, 3 * HD), jnp.float32)
    operands = held_near(*[b for pair in pairs for b in pair])
    operands += [w_qkv] + ([] if before is None else held_near(before))
    outs = [
        pltpu.VMEM((FT, HD), jnp.bfloat16),
        pltpu.VMEM((FT, 2 * HD), jnp.bfloat16),
    ]
    return pl.pallas_call(
        lambda *refs: qkv_body(count, last, *refs),
        in_specs=[pl.BlockSpec(memory_space=pltpu.SMEM)]
        + [pl.BlockSpec(memory_space=pltpu.VMEM)] * len(operands),
        out_shape=outs if last else acc,
        scratch_shapes=([pltpu.VMEM(acc.shape, jnp.float32)] if last else [])
        + [pltpu.VMEM((2 * count, ROWS, HALF), jnp.bfloat16)],
        cost_estimate=pl.CostEstimate(
            flops=2 * count * ROWS * D * 3 * HD, bytes_accessed=6 << 20, transcendentals=0
        ),
        compiler_params=ROOM,
        name="qkv_last" if last else "qkv_add",
    )(table, *operands)


def places(x, y, pieces):
    odd = {"x": x % 2 == 1, "y": y % 2 == 1}
    bits = {"x": (16, 8), "y": (2, 1)}

    def place(axis, piece):
        one, three = bits[axis]
        if piece == 0:
            return 0
        if piece == 3:
            return one + three
        return jnp.where(odd[axis] == (piece == 1), one, three)

    table = []
    for piece in pieces:
        for near, far in (("x", "y"), ("y", "x")):
            for j in range(8):
                table.append(place(far, piece) + place(near, j // 2) + 4 * (j % 2))
    return jnp.stack([jnp.asarray(t, jnp.int32) for t in table])


def attention_body(count, limits, *refs):
    qs, (k0, v0, cache1, kv0, kv1) = refs[:count], refs[count : count + 5]
    outs, stat_ref = refs[count + 5 : 2 * count + 5], refs[-1]
    chunks = []
    for c, (k, v, side) in enumerate(((k0, v0, 0), (cache1, cache1, HD))):
        for at in range(0, k.shape[0], CHUNK):
            chunks.append((k, v, side, at, c))
    chunks.append((None, None, 0, 0, 2))
    rows = 256
    blocks = FT // rows
    ones = jnp.ones((CHUNK, HD), jnp.bfloat16)

    def one_block(index, carry):
        frame = index // blocks
        start = pl.multiple_of((index % blocks) * rows, rows)
        limit = [limits[frame * 4 + c] for c in range(4)]
        any_key = (limit[0] > 0) | (limit[1] > 0) | (limit[2] > 0) | (limit[3] > 0)
        q = qs[0][pl.ds(start, rows), :]
        for f in range(1, count):
            q = jnp.where(frame == f, qs[f][pl.ds(start, rows), :], q)
        peak = jnp.full((rows, 1), NEG, jnp.float32)
        acc = jnp.zeros((rows, 2 * HD), jnp.float32)
        column = lax.broadcasted_iota(jnp.int32, (1, CHUNK), 1)
        for k, v, side, at, c in chunks:
            if k is None:
                keys, values = (
                    jnp.concatenate([kv[:, h : h + HD] for kv in (kv0, kv1)], axis=0)
                    for h in (0, HD)
                )
                inside = column < jnp.where(column < FT, limit[2], FT + limit[3])
            else:
                keys, values = k[at : at + CHUNK, :HD], v[at : at + CHUNK, side : side + HD]
                inside = column < limit[c] - at
            s = lax.dot_general(
                q, keys, (((1,), (1,)), ((), ())), preferred_element_type=jnp.float32
            )
            s = jnp.where(inside, s, NEG)
            newest = jnp.maximum(peak, jnp.max(s, axis=-1, keepdims=True))
            w = jnp.exp2((s - newest) * EXP_SCALE).astype(jnp.bfloat16)
            values = jnp.concatenate([values, ones], axis=1)
            acc = acc * jnp.exp2((peak - newest) * EXP_SCALE) + jnp.dot(
                w, values, preferred_element_type=jnp.float32
            )
            peak = newest
        total = acc[:, HD:]
        result = jnp.where(any_key, acc[:, :HD] / total, 0.0).astype(jnp.bfloat16)
        for f in range(count):

            @pl.when(frame == f)
            def _(f=f):
                outs[f][pl.ds(start, rows), :] = result

        level = jnp.where(any_key, peak * EXP_SCALE + jnp.log2(total), NEG)
        stat_ref[pl.ds(index, 1), :] = level.T[0:1, :]
        return carry

    lax.fori_loop(0, count * blocks, one_block, 0)
    for f in range(count):
        flat = jnp.concatenate(
            [stat_ref[i : i + 1, :] for i in range(f * blocks, (f + 1) * blocks)], axis=1
        )
        lines = []
        for piece in pieces_of(flat):
            for at in range(0, FT, HD):
                lines.append(piece[:, at : at + HD])
        lines.append(jnp.zeros((4, HD), jnp.float32))
        outs[f][FT:, :] = jnp.concatenate(lines, axis=0).astype(jnp.bfloat16)


def attention(limits, qs, k0, v0, cache1, kv0, kv1):
    count = len(qs)
    whole = pl.BlockSpec(memory_space=pltpu.VMEM)
    return pl.pallas_call(
        lambda *refs: attention_body(count, *refs),
        in_specs=[pl.BlockSpec(memory_space=pltpu.SMEM)] + [whole] * (5 + count),
        out_shape=[pltpu.VMEM((PAY, HD), jnp.bfloat16)] * count,
        scratch_shapes=[pltpu.VMEM((8, 256), jnp.float32)],
        cost_estimate=pl.CostEstimate(
            flops=count * 4 * FT * 5120 * HD,
            bytes_accessed=3 << 20,
            transcendentals=count * FT * 5120,
        ),
        compiler_params=ROOM,
        name="attention",
    )(limits, *qs, k0, v0, cache1, kv0, kv1)


def combine_body(*refs):
    parts, o_ref = refs[:-1], refs[-1]
    levels = []
    for part in parts:
        lines = part[FT:, :].astype(jnp.float32)
        level = (lines[0:4] + lines[4:8]) + lines[8:12]
        row = jnp.concatenate([level[i : i + 1, :] for i in range(4)], axis=1)
        levels.append(jnp.broadcast_to(row, (HD, FT)).T)
    peak = levels[0]
    for level in levels[1:]:
        peak = jnp.maximum(peak, level)
    total = jnp.zeros((FT, HD), jnp.float32)
    acc = jnp.zeros((FT, HD), jnp.float32)
    for part, level in zip(parts, levels):
        w = jnp.exp2(level - peak)
        total = total + w
        acc = acc + w * part[:FT, :].astype(jnp.float32)
    o_ref[...] = (acc / total).astype(jnp.bfloat16)


def combine(parts):
    return pl.pallas_call(
        combine_body,
        out_shape=pltpu.VMEM((FT, HD), jnp.bfloat16),
        compiler_params=ROOM,
        name="combine",
    )(*held_near(*parts))


def beside_body(keys_ref, values_ref, out_ref):
    out_ref[:, :HD] = keys_ref[...]
    out_ref[:, HD:] = values_ref[...]


def beside(keys, values):
    return pl.pallas_call(
        beside_body,
        out_shape=pltpu.VMEM((keys.shape[0], 2 * HD), keys.dtype),
        compiler_params=ROOM,
        name="beside",
    )(keys, values)


def insert_body(offset_ref, root_ref, k_ref, v_ref, new_k_ref, new_v_ref, rolled_ref):
    new_k_ref[...] = k_ref[...]
    new_v_ref[...] = v_ref[...]
    offset = offset_ref[0]
    rest = offset & (TOK - 1)
    base = offset - rest
    rows = jnp.concatenate(
        [root_ref[...].astype(jnp.float32), jnp.zeros((TOK, 2 * HD), jnp.float32)], axis=0
    )
    rolled_ref[...] = pltpu.roll(rows, rest, 0)

    def one(i, carry):
        start = base + i * TOK

        @pl.when((start >= 0) & (start < k_ref.shape[0]))
        def _():
            at = pl.ds(pl.multiple_of(start, TOK), TOK)
            source = pl.multiple_of(i * TOK, TOK)
            row = source + lax.broadcasted_iota(jnp.int32, (TOK, HD), 0)
            inside = (row >= rest) & (row < rest + FT)
            for c, out in enumerate((new_k_ref, new_v_ref)):
                fresh = rolled_ref[pl.ds(source, TOK), c * HD : (c + 1) * HD]
                out[at, :] = jnp.where(inside, fresh, out[at, :].astype(jnp.float32)).astype(
                    out.dtype
                )

        return carry

    lax.fori_loop(0, FT // TOK + 1, one, 0)


def insert_rows(root, keys, values, offset):
    return pl.pallas_call(
        insert_body,
        in_specs=[pl.BlockSpec(memory_space=pltpu.SMEM)]
        + [pl.BlockSpec(memory_space=pltpu.VMEM)] * 3,
        out_shape=[jax.ShapeDtypeStruct(keys.shape, keys.dtype)] * 2,
        scratch_shapes=[pltpu.VMEM((FT + TOK, 2 * HD), jnp.float32)],
        compiler_params=ROOM,
        name="insert_rows",
    )(offset, *held_near(root), keys, values)


def order_body(table, own_ref, other_ref, first_ref, second_ref, out_ref):
    slot = table[32]
    for source, chosen in (
        (own_ref, slot == 0),
        (other_ref, slot == 1),
        (first_ref, (slot == 2) | (slot == 7)),
        (second_ref, (slot > 2) & (slot < 7)),
    ):

        @pl.when(chosen)
        def _(source=source):
            for j in range(32):
                at = pl.multiple_of(table[j] * TOK, TOK)
                out_ref[j * TOK : (j + 1) * TOK, :] = source[pl.ds(at, TOK), :]


def token_places(slot, x, zl, y):
    block = jnp.arange(32, dtype=jnp.int32)

    def pair(apart):
        three = (apart >> 1) & 1
        return ((apart ^ (3 * three)) & 1) * 2 + three

    place = (
        pair((block >> 3) ^ x) * 8 + (((block >> 2) & 1) ^ zl) * 4 + pair((block & 3) ^ y)
    )
    return jnp.concatenate([place, slot.reshape(1)]).astype(jnp.int32)


def in_token_order(table, own, other, first, second):
    return pl.pallas_call(
        order_body,
        in_specs=[pl.BlockSpec(memory_space=pltpu.SMEM)]
        + [pl.BlockSpec(memory_space=pltpu.VMEM)] * 4,
        out_shape=pltpu.VMEM(own.shape, own.dtype),
        compiler_params=ROOM,
        name="in_token_order",
    )(table, own, other, first, second)


def relay_body(slot_ref, own_ref, other_ref, got_ref, out_ref):
    for source, chosen in (
        (own_ref, slot_ref[0] == 0),
        (other_ref, slot_ref[0] == 1),
        (got_ref, slot_ref[0] > 1),
    ):

        @pl.when(chosen)
        def _(source=source):
            out_ref[...] = source[...]


def relay(slot, own, other, got):
    return pl.pallas_call(
        relay_body,
        in_specs=[pl.BlockSpec(memory_space=pltpu.SMEM)]
        + [pl.BlockSpec(memory_space=pltpu.VMEM)] * 3,
        out_shape=pltpu.VMEM(own.shape, own.dtype),
        compiler_params=ROOM,
        name="relay",
    )(slot, own, other, got)


REDUCE = ((2, 3), (3, 4), (4, 2))


def stack_body(*refs):
    for i in range(3):
        refs[3][i * HD : (i + 1) * HD, :] = refs[i][...]


def stack(blocks):
    return pl.pallas_call(
        stack_body,
        out_shape=pltpu.VMEM((3 * HD, HALF), jnp.bfloat16),
        compiler_params=ROOM,
        name="stack",
    )(*held_near(*blocks))


def out_body(order, t0, t1, t2, t3, n0, n1, n2, n3, f0, f1, keep_ref, send_ref, lhs_ref):
    for b in range(8):
        block = pl.multiple_of(order[b] * TOK, TOK)
        lhs_ref[b * TOK : (b + 1) * TOK, :] = jnp.concatenate(
            [t[pl.ds(block, TOK), :] for t in (t0, t1, t2, t3)], axis=1
        )
    for c, side in enumerate(((n0, n1, n2, n3), (f0, f1))):
        columns = slice(c * HALF, (c + 1) * HALF)
        weights = jnp.concatenate([w[...] for w in side], axis=0)
        product = jnp.dot(lhs_ref[...], weights, preferred_element_type=jnp.float32)
        keep_ref[:, columns] = product[: ROWS // 2].astype(jnp.bfloat16)
        send_ref[:, columns] = product[ROWS // 2 :].astype(jnp.bfloat16)


def out_project(order, tokens, sides):
    return pl.pallas_call(
        out_body,
        in_specs=[pl.BlockSpec(memory_space=pltpu.SMEM)]
        + [pl.BlockSpec(memory_space=pltpu.VMEM)] * 10,
        out_shape=[pltpu.VMEM((ROWS // 2, D), jnp.bfloat16)] * 2,
        scratch_shapes=[pltpu.VMEM((ROWS, 4 * HD), jnp.bfloat16)],
        compiler_params=ROOM,
        name="out_project",
    )(order, *held_near(*tokens), *sides)


def add_body(keep_ref, got_ref, next_keep_ref, next_send_ref):
    total = keep_ref[...].astype(jnp.float32) + got_ref[...].astype(jnp.float32)
    rows = total.shape[0] // 2
    next_keep_ref[...] = total[:rows].astype(jnp.bfloat16)
    next_send_ref[...] = total[rows:].astype(jnp.bfloat16)


def add_up(keep, got):
    shape = pltpu.VMEM((keep.shape[0] // 2, D), jnp.bfloat16)
    return pl.pallas_call(
        add_body, out_shape=[shape] * 2, compiler_params=ROOM, name="add_up"
    )(*held_near(keep, got))


def finish_body(core_ref, keep_ref, got_ref, carry_ref, out_ref):
    total = keep_ref[...].astype(jnp.float32) + got_ref[...].astype(jnp.float32)
    near, far = total[:, :HALF], total[:, HALF:]
    lines = carry_ref[TOK:, :].astype(jnp.float32)
    gate = (lines[0:1] + lines[1:2]) + lines[2:3]
    base = carry_ref[:TOK, :].astype(jnp.float32)
    first = core_ref[0] == 0
    for h, product in ((0, jnp.where(first, near, far)), (1, jnp.where(first, far, near))):
        columns = slice(h * HALF, (h + 1) * HALF)
        out_ref[:, columns] = (base[:, columns] + gate[:, columns] * product).astype(jnp.bfloat16)


def finish(core, keep, got, carry):
    return pl.pallas_call(
        finish_body,
        in_specs=[pl.BlockSpec(memory_space=pltpu.SMEM)]
        + [pl.BlockSpec(memory_space=pltpu.VMEM)] * 3,
        out_shape=pltpu.VMEM((TOK, D), jnp.bfloat16),
        compiler_params=ROOM,
        name="finish",
    )(core, *held_near(keep, got, carry))


def step(
    window,
    levels,
    actions,
    cache_len,
    level_table,
    action_table,
    w_qkv,
    w_out,
    cache_keys,
    cache_values,
    fresh_frame,
):
    core = lax.axis_index("core")
    slot = lax.axis_index(FRAME)
    length = cache_len[0]
    shard_rows = cache_keys.shape[0]

    condition = (
        lax.dynamic_slice_in_dim(level_table, levels[0], 1, 0)
        + lax.dynamic_slice_in_dim(action_table, actions[0], 1, 0)
    )[0]
    normed, carry = normalise(window, condition)

    got = across(normed, 2)

    places_here = [lax.axis_index(a).astype(jnp.int32) for a in FSDP]
    slot, core, length, w_late, x, zl, y, _ = lax.optimization_barrier(
        (slot, core, length, w_out, *places_here, normed)
    )
    slots = slot.astype(jnp.int32).reshape(1)
    cores = core.astype(jnp.int32).reshape(1)
    offset = (length - slot * shard_rows).astype(jnp.int32)
    w_near = lax.dynamic_slice_in_dim(w_late, core * HALF, HALF, 1)
    w_far = lax.dynamic_slice_in_dim(w_late, (1 - core) * HALF, HALF, 1)

    def limits(*ahead):
        rows = []
        for steps in ahead:
            frame = (slot + steps) % 8
            partner = slot ^ 1
            rows += [
                length - slot * shard_rows,
                length - partner * shard_rows,
                jnp.where(slot <= frame, FT, 0),
                jnp.where(partner <= frame, FT, 0),
            ]
        return jnp.stack(rows).astype(jnp.int32)

    tables = [places(x, y, p) for p in ((0,), (1, 2), (3,))]
    tables += [limits(0), limits(2, 6), limits(4), token_places(slots[0], x, zl, y)]
    tables += [
        jnp.where(
            core == 0,
            jnp.arange(8, dtype=jnp.int32),
            jnp.array([(b & 1) * 4 + (b >> 1) for b in range(8)], jnp.int32),
        ),
        jnp.clip(offset, -FT, shard_rows).reshape(1),
        cores,
        slots,
    ]
    got, w_near, w_far, *tables = lax.optimization_barrier((got, w_near, w_far, *tables))
    order, offset, cores, slots = tables[7:]
    first, second = halves(normed, got)
    first, second = join((first, *ring(first, "x", cores)), (second, *ring(second, "y", cores)))

    late = lax.optimization_barrier((first, second, cache_keys, cache_values))
    first, second = late[:2]
    other_cache = other_core(beside(late[2], late[3]))

    around = list(zip(ring(first, "y", cores), ring(second, "x", cores)))
    acc = qkv_add(tables[0], [(first, second)], w_qkv, None, False)
    acc = qkv_add(tables[1], around[:2], w_qkv, acc, False)
    acc, opposite, other_cache = lax.optimization_barrier((acc, around[2], other_cache))
    query, key_value = qkv_add(tables[2], [opposite], w_qkv, acc, True)

    q_up = frame_shift(query, -2)
    q_down = frame_shift(query, 2)
    q_far = frame_shift(query, 4)
    other_key_value = other_core(key_value)

    def attend(table, *queries):
        return attention(
            table,
            queries,
            cache_keys,
            cache_values,
            other_cache,
            key_value,
            other_key_value,
        )

    (part,) = attend(tables[3], query)
    part, q_up, q_down, w_next, carry = lax.optimization_barrier(
        (part, q_up, q_down, w_near, carry)
    )
    sent = [frame_shift(part, -1)]
    w_one, w_three = across(w_next, 0), across(w_next, 1)
    other_late = after(other_key_value, part)
    root_first = lax.ppermute(
        relay(slots, key_value, other_late, key_value), FRAME, [(0, 2), (1, 7)]
    )
    part_up, part_down = attend(tables[4], q_up, q_down)
    sent.append(frame_shift(part_up, 1))
    sent.append(frame_shift(part_down, -3))
    part_up, q_far, w_one, w_three, root_first = lax.optimization_barrier(
        (part_up, q_far, w_one, w_three, root_first)
    )
    w_two = by_core(pick(cores, w_one, w_three), "x", (lambda i: i ^ 3, lambda i: i ^ 1))
    (part,) = attend(tables[5], q_far)
    sent.append(frame_shift(part, 3))
    part, w_two = lax.optimization_barrier((part, w_two))
    heads_far = other_core(stack((w_one, w_three, w_two)))
    sides = [w_near, w_one, w_three, w_two, w_far, heads_far]
    carry_next = frame_shift(after(carry, part), -1)

    attended = combine(sent).reshape(2, 2, ROWS, HD)

    beyond = lax.ppermute(attended[1, 1], "x", [(i, i ^ 2) for i in range(4)])
    together = [attended[0, 0], across(attended[1, 0], 0), across(attended[0, 1], 1), beyond]
    keep, send = out_project(order, together, sides)
    got = across_each(send, REDUCE[0])
    root_second = lax.ppermute(
        relay(slots, key_value, other_key_value, after(root_first, send)),
        FRAME,
        [(0, 4), (1, 5), (2, 3), (7, 6)],
    )
    keep, send = add_up(keep, got)
    got = across_each(send, REDUCE[1])
    got, root_second = lax.optimization_barrier((got, root_second))
    keep, send = add_up(keep, got)
    got = across_each(send, REDUCE[2])
    root = in_token_order(tables[6], key_value, other_key_value, root_first, root_second)
    got, root = lax.optimization_barrier((got, root))
    updated = finish(cores, keep, got, carry_next)

    next_window = jnp.where(slot == 7, fresh_frame, updated)
    arrived = [lax.ppermute(updated, FRAME, [(7, 2 * chip + 1)]) for chip in (1, 0, 2)]
    new_keys, new_values = insert_rows(
        after(root, updated), cache_keys, cache_values, offset
    )
    arrived, new_keys, new_values = lax.optimization_barrier((arrived, new_keys, new_values))
    finished = jnp.where(slot == 7, updated, arrived[0] + arrived[1] + arrived[2])
    finished = jnp.where(core == 0, lax.ppermute(finished, "core", [(1, 0)]), finished)
    return (next_window[None], finished, new_keys, new_values)


def solution(mesh):
    split = Mesh(mesh.devices.reshape(4, 2, 4, 2, 4), FRAME + FSDP)
    return jax.shard_map(
        step,
        mesh=split,
        in_specs=(
            P(FRAME, FSDP, None),
            P(FRAME),
            P(FRAME),
            P(),
            P(),
            P(),
            P(None, None, FSDP),
            P(FSDP, None),
            P(FRAME, FSDP),
            P(FRAME, FSDP),
            P(FSDP, None),
        ),
        out_specs=(P(FRAME, FSDP, None), P(FSDP, None), P(FRAME, FSDP), P(FRAME, FSDP)),
        check_vma=False,
    )
```

```python
import math

import jax
import jax.numpy as jnp
from jax import lax
from jax.experimental import pallas as pl
from jax.experimental.pallas import tpu as pltpu
from jax.sharding import Mesh
from jax.sharding import PartitionSpec as P

HD = 128
D = 5120
FT = 512
TOK = 16
ROWS = FT // 4
HALF = D // 2
EPS = 1e-06
NEG = -1e30
LOG2E = math.log2(math.e)
EXP_SCALE = LOG2E / math.sqrt(HD)
CHUNK = 1024
PAY = FT + 16

FRAME = ("zh", "core")
FSDP = ("x", "zl", "y")

ROOM = pltpu.CompilerParams(vmem_limit_bytes=18 << 20)


DIMS = (("x", 1, 4), ("x", 3, 4), ("zl", 1, 2), ("y", 1, 4), ("y", 3, 4))


def held_near(*blocks):
    return [pltpu.with_memory_space_constraint(b, pltpu.VMEM) for b in blocks]


def across(block, dim):
    axis, mask, size = DIMS[dim]
    return lax.ppermute(block, axis, [(i, i ^ mask) for i in range(size)])


def across_each(block, by_core):
    pairs = []
    for core in range(2):
        axis, mask, _ = DIMS[by_core[core]]
        for x in range(4):
            for zl in range(2):
                for y in range(4):
                    at = {"x": x, "zl": zl, "y": y}
                    to = dict(at, **{axis: at[axis] ^ mask})
                    pairs.append(
                        tuple(((core * 4 + p["x"]) * 2 + p["zl"]) * 4 + p["y"] for p in (at, to))
                    )
    return lax.ppermute(block, ("core", "x", "zl", "y"), pairs)


def frame_shift(block, distance):
    return lax.ppermute(block, FRAME, [(i, (i + distance) % 8) for i in range(8)])


def other_core(block):
    return lax.ppermute(block, "core", [(0, 1), (1, 0)])


def pieces_of(value):
    high = value.astype(jnp.bfloat16).astype(jnp.float32)
    rest = value - high
    middle = rest.astype(jnp.bfloat16).astype(jnp.float32)
    return high, middle, rest - middle


def norm_body(window_ref, condition_ref, out_ref, carry_ref):
    rows = window_ref[0].astype(jnp.float32)
    center = rows - jnp.mean(rows, axis=-1, keepdims=True)
    spread = jnp.mean(center * center, axis=-1, keepdims=True)
    out_ref[...] = (
        center * lax.rsqrt(spread + EPS) * (1.0 + condition_ref[1:2, :]) + condition_ref[0:1, :]
    ).astype(jnp.bfloat16)
    carry_ref[:TOK, :] = window_ref[0]
    gate = pieces_of(condition_ref[2:3, :])
    empty = jnp.zeros((TOK - 3, D), jnp.float32)
    carry_ref[TOK:, :] = jnp.concatenate([*gate, empty], axis=0).astype(jnp.bfloat16)


def normalise(window, condition):
    return pl.pallas_call(
        norm_body,
        out_shape=[
            pltpu.VMEM((TOK, D), jnp.bfloat16),
            pltpu.VMEM((2 * TOK, D), jnp.bfloat16),
        ],
        compiler_params=ROOM,
        name="normalise",
    )(window, condition)


def halves_body(*refs):
    blocks, outs = refs[:-2], refs[-2:]
    for i, block in enumerate(blocks):
        for h in range(2):
            outs[h][i * TOK : (i + 1) * TOK, :] = block[:, h * HALF : (h + 1) * HALF]


def halves(mine, got):
    return pl.pallas_call(
        halves_body,
        out_shape=[pltpu.VMEM((2 * TOK, HALF), jnp.bfloat16)] * 2,
        compiler_params=ROOM,
        name="halves",
    )(*held_near(mine, got))


def join_body(*refs):
    rows = refs[0].shape[0]
    for h in range(2):
        for i in range(4):
            refs[8 + h][i * rows : (i + 1) * rows, :] = refs[4 * h + i][...]


def join(first, second):
    shape = pltpu.VMEM((4 * first[0].shape[0], HALF), jnp.bfloat16)
    return pl.pallas_call(
        join_body, out_shape=[shape] * 2, compiler_params=ROOM, name="join"
    )(*held_near(*first, *second))


def after(block, *earlier):
    return lax.optimization_barrier((block, *earlier))[0]


def pick_body(core_ref, first_ref, second_ref, out_ref):
    @pl.when(core_ref[0] == 0)
    def _():
        out_ref[...] = first_ref[...]

    @pl.when(core_ref[0] != 0)
    def _():
        out_ref[...] = second_ref[...]


def pick(core, first, second):
    return pl.pallas_call(
        pick_body,
        in_specs=[pl.BlockSpec(memory_space=pltpu.SMEM)]
        + [pl.BlockSpec(memory_space=pltpu.VMEM)] * 2,
        out_shape=pltpu.VMEM(first.shape, first.dtype),
        compiler_params=ROOM,
        name="pick",
    )(core, *held_near(first, second))


def by_core(block, axis, routes):
    pairs = [(c * 4 + i, c * 4 + routes[c](i)) for c in range(2) for i in range(4)]
    return lax.ppermute(block, ("core", axis), pairs)


def ring(block, axis, core):
    before = lax.ppermute(block, axis, [(i, (i + 1) % 4) for i in range(4)])
    behind = lax.ppermute(block, axis, [(i, (i - 1) % 4) for i in range(4)])
    opposite = by_core(
        pick(core, before, behind), axis, (lambda i: (i + 1) % 4, lambda i: (i - 1) % 4)
    )
    return before, behind, opposite


def qkv_body(count, last, table, *refs):
    blocks, w_ref, refs, x_ref = refs[: 2 * count], refs[2 * count], refs[2 * count + 1 : -1], refs[-1]
    if last:
        before_ref, query_ref, key_value_ref, acc_ref = refs
    elif len(refs) == 2:
        before_ref, acc_ref = refs
    else:
        before_ref, acc_ref = None, refs[0]
    if before_ref is None:
        acc_ref[...] = jnp.zeros(acc_ref.shape, jnp.float32)
    else:
        acc_ref[...] = before_ref[...]
    for i in range(2 * count):
        x_ref[i] = blocks[i][...]

    def one(i, carry):
        at = pl.multiple_of((i % 2) * HALF, HALF)
        w = jnp.concatenate([w_ref[c, pl.ds(at, HALF), :] for c in range(3)], axis=1)
        product = jnp.dot(x_ref[i], w, preferred_element_type=jnp.float32)
        for j in range(8):
            at = pl.multiple_of(table[i * 8 + j] * TOK, TOK)
            acc_ref[pl.ds(at, TOK), :] += product[j * TOK : (j + 1) * TOK, :]
        return carry

    lax.fori_loop(0, 2 * count, one, 0)
    if last:
        query_ref[...] = acc_ref[:, :HD].astype(jnp.bfloat16)
        key_value_ref[...] = acc_ref[:, HD:].astype(jnp.bfloat16)


def qkv_add(table, pairs, w_qkv, before, last):
    count = len(pairs)
    acc = pltpu.VMEM((FT, 3 * HD), jnp.float32)
    operands = held_near(*[b for pair in pairs for b in pair])
    operands += [w_qkv] + ([] if before is None else held_near(before))
    outs = [
        pltpu.VMEM((FT, HD), jnp.bfloat16),
        pltpu.VMEM((FT, 2 * HD), jnp.bfloat16),
    ]
    return pl.pallas_call(
        lambda *refs: qkv_body(count, last, *refs),
        in_specs=[pl.BlockSpec(memory_space=pltpu.SMEM)]
        + [pl.BlockSpec(memory_space=pltpu.VMEM)] * len(operands),
        out_shape=outs if last else acc,
        scratch_shapes=([pltpu.VMEM(acc.shape, jnp.float32)] if last else [])
        + [pltpu.VMEM((2 * count, ROWS, HALF), jnp.bfloat16)],
        cost_estimate=pl.CostEstimate(
            flops=2 * count * ROWS * D * 3 * HD, bytes_accessed=6 << 20, transcendentals=0
        ),
        compiler_params=ROOM,
        name="qkv_last" if last else "qkv_add",
    )(table, *operands)


def places(x, y, pieces):
    odd = {"x": x % 2 == 1, "y": y % 2 == 1}
    bits = {"x": (16, 8), "y": (2, 1)}

    def place(axis, piece):
        one, three = bits[axis]
        if piece == 0:
            return 0
        if piece == 3:
            return one + three
        return jnp.where(odd[axis] == (piece == 1), one, three)

    table = []
    for piece in pieces:
        for near, far in (("x", "y"), ("y", "x")):
            for j in range(8):
                table.append(place(far, piece) + place(near, j // 2) + 4 * (j % 2))
    return jnp.stack([jnp.asarray(t, jnp.int32) for t in table])


def attention_body(count, limits, *refs):
    qs, (k0, v0, cache1, kv0, kv1) = refs[:count], refs[count : count + 5]
    outs, stat_ref = refs[count + 5 : 2 * count + 5], refs[-1]
    chunks = []
    for c, (k, v, side) in enumerate(((k0, v0, 0), (cache1, cache1, HD))):
        for at in range(0, k.shape[0], CHUNK):
            chunks.append((k, v, side, at, c))
    chunks.append((None, None, 0, 0, 2))
    rows = 256
    blocks = FT // rows
    ones = jnp.ones((CHUNK, HD), jnp.bfloat16)

    def one_block(index, carry):
        frame = index // blocks
        start = pl.multiple_of((index % blocks) * rows, rows)
        limit = [limits[frame * 4 + c] for c in range(4)]
        any_key = (limit[0] > 0) | (limit[1] > 0) | (limit[2] > 0) | (limit[3] > 0)
        q = qs[0][pl.ds(start, rows), :]
        for f in range(1, count):
            q = jnp.where(frame == f, qs[f][pl.ds(start, rows), :], q)
        peak = jnp.full((rows, 1), NEG, jnp.float32)
        acc = jnp.zeros((rows, 2 * HD), jnp.float32)
        column = lax.broadcasted_iota(jnp.int32, (1, CHUNK), 1)
        for k, v, side, at, c in chunks:
            if k is None:
                keys, values = (
                    jnp.concatenate([kv[:, h : h + HD] for kv in (kv0, kv1)], axis=0)
                    for h in (0, HD)
                )
                inside = column < jnp.where(column < FT, limit[2], FT + limit[3])
            else:
                keys, values = k[at : at + CHUNK, :HD], v[at : at + CHUNK, side : side + HD]
                inside = column < limit[c] - at
            s = lax.dot_general(
                q, keys, (((1,), (1,)), ((), ())), preferred_element_type=jnp.float32
            )
            s = jnp.where(inside, s, NEG)
            newest = jnp.maximum(peak, jnp.max(s, axis=-1, keepdims=True))
            w = jnp.exp2((s - newest) * EXP_SCALE).astype(jnp.bfloat16)
            values = jnp.concatenate([values, ones], axis=1)
            acc = acc * jnp.exp2((peak - newest) * EXP_SCALE) + jnp.dot(
                w, values, preferred_element_type=jnp.float32
            )
            peak = newest
        total = acc[:, HD:]
        result = jnp.where(any_key, acc[:, :HD] / total, 0.0).astype(jnp.bfloat16)
        for f in range(count):

            @pl.when(frame == f)
            def _(f=f):
                outs[f][pl.ds(start, rows), :] = result

        level = jnp.where(any_key, peak * EXP_SCALE + jnp.log2(total), NEG)
        stat_ref[pl.ds(index, 1), :] = level.T[0:1, :]
        return carry

    lax.fori_loop(0, count * blocks, one_block, 0)
    for f in range(count):
        flat = jnp.concatenate(
            [stat_ref[i : i + 1, :] for i in range(f * blocks, (f + 1) * blocks)], axis=1
        )
        lines = []
        for piece in pieces_of(flat):
            for at in range(0, FT, HD):
                lines.append(piece[:, at : at + HD])
        lines.append(jnp.zeros((4, HD), jnp.float32))
        outs[f][FT:, :] = jnp.concatenate(lines, axis=0).astype(jnp.bfloat16)


def attention(limits, qs, k0, v0, cache1, kv0, kv1):
    count = len(qs)
    whole = pl.BlockSpec(memory_space=pltpu.VMEM)
    return pl.pallas_call(
        lambda *refs: attention_body(count, *refs),
        in_specs=[pl.BlockSpec(memory_space=pltpu.SMEM)] + [whole] * (5 + count),
        out_shape=[pltpu.VMEM((PAY, HD), jnp.bfloat16)] * count,
        scratch_shapes=[pltpu.VMEM((8, 256), jnp.float32)],
        cost_estimate=pl.CostEstimate(
            flops=count * 4 * FT * 5120 * HD,
            bytes_accessed=3 << 20,
            transcendentals=count * FT * 5120,
        ),
        compiler_params=ROOM,
        name="attention",
    )(limits, *qs, k0, v0, cache1, kv0, kv1)


def combine_body(*refs):
    parts, o_ref = refs[:-1], refs[-1]
    levels = []
    for part in parts:
        lines = part[FT:, :].astype(jnp.float32)
        level = (lines[0:4] + lines[4:8]) + lines[8:12]
        row = jnp.concatenate([level[i : i + 1, :] for i in range(4)], axis=1)
        levels.append(jnp.broadcast_to(row, (HD, FT)).T)
    peak = levels[0]
    for level in levels[1:]:
        peak = jnp.maximum(peak, level)
    total = jnp.zeros((FT, HD), jnp.float32)
    acc = jnp.zeros((FT, HD), jnp.float32)
    for part, level in zip(parts, levels):
        w = jnp.exp2(level - peak)
        total = total + w
        acc = acc + w * part[:FT, :].astype(jnp.float32)
    o_ref[...] = (acc / total).astype(jnp.bfloat16)


def combine(parts):
    return pl.pallas_call(
        combine_body,
        out_shape=pltpu.VMEM((FT, HD), jnp.bfloat16),
        compiler_params=ROOM,
        name="combine",
    )(*held_near(*parts))


def beside_body(keys_ref, values_ref, out_ref):
    out_ref[:, :HD] = keys_ref[...]
    out_ref[:, HD:] = values_ref[...]


def beside(keys, values):
    return pl.pallas_call(
        beside_body,
        out_shape=pltpu.VMEM((keys.shape[0], 2 * HD), keys.dtype),
        compiler_params=ROOM,
        name="beside",
    )(keys, values)


def insert_body(offset_ref, root_ref, k_ref, v_ref, new_k_ref, new_v_ref, rolled_ref):
    new_k_ref[...] = k_ref[...]
    new_v_ref[...] = v_ref[...]
    offset = offset_ref[0]
    rest = offset & (TOK - 1)
    base = offset - rest
    rows = jnp.concatenate(
        [root_ref[...].astype(jnp.float32), jnp.zeros((TOK, 2 * HD), jnp.float32)], axis=0
    )
    rolled_ref[...] = pltpu.roll(rows, rest, 0)

    def one(i, carry):
        start = base + i * TOK

        @pl.when((start >= 0) & (start < k_ref.shape[0]))
        def _():
            at = pl.ds(pl.multiple_of(start, TOK), TOK)
            source = pl.multiple_of(i * TOK, TOK)
            row = source + lax.broadcasted_iota(jnp.int32, (TOK, HD), 0)
            inside = (row >= rest) & (row < rest + FT)
            for c, out in enumerate((new_k_ref, new_v_ref)):
                fresh = rolled_ref[pl.ds(source, TOK), c * HD : (c + 1) * HD]
                out[at, :] = jnp.where(inside, fresh, out[at, :].astype(jnp.float32)).astype(
                    out.dtype
                )

        return carry

    lax.fori_loop(0, FT // TOK + 1, one, 0)


def insert_rows(root, keys, values, offset):
    return pl.pallas_call(
        insert_body,
        in_specs=[pl.BlockSpec(memory_space=pltpu.SMEM)]
        + [pl.BlockSpec(memory_space=pltpu.VMEM)] * 3,
        out_shape=[jax.ShapeDtypeStruct(keys.shape, keys.dtype)] * 2,
        scratch_shapes=[pltpu.VMEM((FT + TOK, 2 * HD), jnp.float32)],
        compiler_params=ROOM,
        name="insert_rows",
    )(offset, *held_near(root), keys, values)


def order_body(table, own_ref, other_ref, first_ref, second_ref, out_ref):
    slot = table[32]
    for source, chosen in (
        (own_ref, slot == 0),
        (other_ref, slot == 1),
        (first_ref, (slot == 2) | (slot == 7)),
        (second_ref, (slot > 2) & (slot < 7)),
    ):

        @pl.when(chosen)
        def _(source=source):
            for j in range(32):
                at = pl.multiple_of(table[j] * TOK, TOK)
                out_ref[j * TOK : (j + 1) * TOK, :] = source[pl.ds(at, TOK), :]


def token_places(slot, x, zl, y):
    block = jnp.arange(32, dtype=jnp.int32)

    def pair(apart):
        three = (apart >> 1) & 1
        return ((apart ^ (3 * three)) & 1) * 2 + three

    place = (
        pair((block >> 3) ^ x) * 8 + (((block >> 2) & 1) ^ zl) * 4 + pair((block & 3) ^ y)
    )
    return jnp.concatenate([place, slot.reshape(1)]).astype(jnp.int32)


def in_token_order(table, own, other, first, second):
    return pl.pallas_call(
        order_body,
        in_specs=[pl.BlockSpec(memory_space=pltpu.SMEM)]
        + [pl.BlockSpec(memory_space=pltpu.VMEM)] * 4,
        out_shape=pltpu.VMEM(own.shape, own.dtype),
        compiler_params=ROOM,
        name="in_token_order",
    )(table, own, other, first, second)


def relay_body(slot_ref, own_ref, other_ref, got_ref, out_ref):
    for source, chosen in (
        (own_ref, slot_ref[0] == 0),
        (other_ref, slot_ref[0] == 1),
        (got_ref, slot_ref[0] > 1),
    ):

        @pl.when(chosen)
        def _(source=source):
            out_ref[...] = source[...]


def relay(slot, own, other, got):
    return pl.pallas_call(
        relay_body,
        in_specs=[pl.BlockSpec(memory_space=pltpu.SMEM)]
        + [pl.BlockSpec(memory_space=pltpu.VMEM)] * 3,
        out_shape=pltpu.VMEM(own.shape, own.dtype),
        compiler_params=ROOM,
        name="relay",
    )(slot, own, other, got)


REDUCE = ((2, 3), (3, 4), (4, 2))


def stack_body(*refs):
    for i in range(3):
        refs[3][i * HD : (i + 1) * HD, :] = refs[i][...]


def stack(blocks):
    return pl.pallas_call(
        stack_body,
        out_shape=pltpu.VMEM((3 * HD, HALF), jnp.bfloat16),
        compiler_params=ROOM,
        name="stack",
    )(*held_near(*blocks))


def out_body(order, t0, t1, t2, t3, n0, n1, n2, n3, f0, f1, keep_ref, send_ref, lhs_ref):
    for b in range(8):
        block = pl.multiple_of(order[b] * TOK, TOK)
        lhs_ref[b * TOK : (b + 1) * TOK, :] = jnp.concatenate(
            [t[pl.ds(block, TOK), :] for t in (t0, t1, t2, t3)], axis=1
        )
    for c, side in enumerate(((n0, n1, n2, n3), (f0, f1))):
        columns = slice(c * HALF, (c + 1) * HALF)
        weights = jnp.concatenate([w[...] for w in side], axis=0)
        product = jnp.dot(lhs_ref[...], weights, preferred_element_type=jnp.float32)
        keep_ref[:, columns] = product[: ROWS // 2].astype(jnp.bfloat16)
        send_ref[:, columns] = product[ROWS // 2 :].astype(jnp.bfloat16)


def out_project(order, tokens, sides):
    return pl.pallas_call(
        out_body,
        in_specs=[pl.BlockSpec(memory_space=pltpu.SMEM)]
        + [pl.BlockSpec(memory_space=pltpu.VMEM)] * 10,
        out_shape=[pltpu.VMEM((ROWS // 2, D), jnp.bfloat16)] * 2,
        scratch_shapes=[pltpu.VMEM((ROWS, 4 * HD), jnp.bfloat16)],
        compiler_params=ROOM,
        name="out_project",
    )(order, *held_near(*tokens), *sides)


def add_body(keep_ref, got_ref, next_keep_ref, next_send_ref):
    total = keep_ref[...].astype(jnp.float32) + got_ref[...].astype(jnp.float32)
    rows = total.shape[0] // 2
    next_keep_ref[...] = total[:rows].astype(jnp.bfloat16)
    next_send_ref[...] = total[rows:].astype(jnp.bfloat16)


def add_up(keep, got):
    shape = pltpu.VMEM((keep.shape[0] // 2, D), jnp.bfloat16)
    return pl.pallas_call(
        add_body, out_shape=[shape] * 2, compiler_params=ROOM, name="add_up"
    )(*held_near(keep, got))


def finish_body(core_ref, keep_ref, got_ref, carry_ref, out_ref):
    total = keep_ref[...].astype(jnp.float32) + got_ref[...].astype(jnp.float32)
    near, far = total[:, :HALF], total[:, HALF:]
    lines = carry_ref[TOK:, :].astype(jnp.float32)
    gate = (lines[0:1] + lines[1:2]) + lines[2:3]
    base = carry_ref[:TOK, :].astype(jnp.float32)
    first = core_ref[0] == 0
    for h, product in ((0, jnp.where(first, near, far)), (1, jnp.where(first, far, near))):
        columns = slice(h * HALF, (h + 1) * HALF)
        out_ref[:, columns] = (base[:, columns] + gate[:, columns] * product).astype(jnp.bfloat16)


def finish(core, keep, got, carry):
    return pl.pallas_call(
        finish_body,
        in_specs=[pl.BlockSpec(memory_space=pltpu.SMEM)]
        + [pl.BlockSpec(memory_space=pltpu.VMEM)] * 3,
        out_shape=pltpu.VMEM((TOK, D), jnp.bfloat16),
        compiler_params=ROOM,
        name="finish",
    )(core, *held_near(keep, got, carry))


def step(
    window,
    levels,
    actions,
    cache_len,
    level_table,
    action_table,
    w_qkv,
    w_out,
    cache_keys,
    cache_values,
    fresh_frame,
):
    core = lax.axis_index("core")
    slot = lax.axis_index(FRAME)
    length = cache_len[0]
    shard_rows = cache_keys.shape[0]

    condition = (
        lax.dynamic_slice_in_dim(level_table, levels[0], 1, 0)
        + lax.dynamic_slice_in_dim(action_table, actions[0], 1, 0)
    )[0]
    normed, carry = normalise(window, condition)

    got = across(normed, 2)

    places_here = [lax.axis_index(a).astype(jnp.int32) for a in FSDP]
    slot, core, length, w_late, x, zl, y, _ = lax.optimization_barrier(
        (slot, core, length, w_out, *places_here, normed)
    )
    slots = slot.astype(jnp.int32).reshape(1)
    cores = core.astype(jnp.int32).reshape(1)
    offset = (length - slot * shard_rows).astype(jnp.int32)
    w_near = lax.dynamic_slice_in_dim(w_late, core * HALF, HALF, 1)
    w_far = lax.dynamic_slice_in_dim(w_late, (1 - core) * HALF, HALF, 1)

    def limits(*ahead):
        rows = []
        for steps in ahead:
            frame = (slot + steps) % 8
            partner = slot ^ 1
            rows += [
                length - slot * shard_rows,
                length - partner * shard_rows,
                jnp.where(slot <= frame, FT, 0),
                jnp.where(partner <= frame, FT, 0),
            ]
        return jnp.stack(rows).astype(jnp.int32)

    tables = [places(x, y, p) for p in ((0,), (1, 2), (3,))]
    tables += [limits(0), limits(2, 6), limits(4), token_places(slots[0], x, zl, y)]
    tables += [
        jnp.where(
            core == 0,
            jnp.arange(8, dtype=jnp.int32),
            jnp.array([(b & 1) * 4 + (b >> 1) for b in range(8)], jnp.int32),
        ),
        jnp.clip(offset, -FT, shard_rows).reshape(1),
        cores,
        slots,
    ]
    got, w_near, w_far, *tables = lax.optimization_barrier((got, w_near, w_far, *tables))
    order, offset, cores, slots = tables[7:]
    first, second = halves(normed, got)
    first, second = join((first, *ring(first, "x", cores)), (second, *ring(second, "y", cores)))

    late = lax.optimization_barrier((first, second, cache_keys, cache_values))
    first, second = late[:2]
    other_cache = other_core(beside(late[2], late[3]))

    around = list(zip(ring(first, "y", cores), ring(second, "x", cores)))
    acc = qkv_add(tables[0], [(first, second)], w_qkv, None, False)
    acc = qkv_add(tables[1], around[:2], w_qkv, acc, False)
    acc, opposite, other_cache = lax.optimization_barrier((acc, around[2], other_cache))
    query, key_value = qkv_add(tables[2], [opposite], w_qkv, acc, True)

    q_up = frame_shift(query, -2)
    q_down = frame_shift(query, 2)
    other_key_value = other_core(key_value)

    def attend(table, *queries):
        return attention(
            table,
            queries,
            cache_keys,
            cache_values,
            other_cache,
            key_value,
            other_key_value,
        )

    (part,) = attend(tables[3], query)
    part, query_late, w_next = lax.optimization_barrier((part, query, w_near))
    q_far = frame_shift(query_late, 4)
    sent = [frame_shift(part, -1)]
    w_one = across(w_next, 0)
    w_three = across(w_next, 1)
    other_late = after(other_key_value, part)
    root_first = lax.ppermute(
        relay(slots, key_value, other_late, key_value), FRAME, [(0, 2), (1, 7)]
    )
    part_up, part_down = attend(tables[4], q_up, q_down)
    sent.append(frame_shift(part_up, 1))
    sent.append(frame_shift(part_down, -3))
    part_up, q_far, w_one, w_three, root_first = lax.optimization_barrier(
        (part_up, q_far, w_one, w_three, root_first)
    )
    w_two = by_core(pick(cores, w_one, w_three), "x", (lambda i: i ^ 3, lambda i: i ^ 1))
    (part,) = attend(tables[5], q_far)
    sent.append(frame_shift(part, 3))
    part, w_two = lax.optimization_barrier((part, w_two))
    heads_far = other_core(stack((w_one, w_three, w_two)))
    sides = [w_near, w_one, w_three, w_two, w_far, heads_far]
    carry_next = frame_shift(after(carry, part), -1)

    attended = combine(sent).reshape(2, 2, ROWS, HD)

    beyond = lax.ppermute(attended[1, 1], "x", [(i, i ^ 2) for i in range(4)])
    together = [attended[0, 0], across(attended[1, 0], 0), across(attended[0, 1], 1), beyond]
    keep, send = out_project(order, together, sides)
    got = across_each(send, REDUCE[0])
    relayed = relay(slots, key_value, other_key_value, after(root_first, send))
    root_second = lax.ppermute(relayed, FRAME, [(0, 4), (1, 5), (2, 3), (7, 6)])
    keep, send = add_up(keep, got)
    got = across_each(send, REDUCE[1])
    got, root_second = lax.optimization_barrier((got, root_second))
    keep, send = add_up(keep, got)
    got = across_each(send, REDUCE[2])
    root = in_token_order(tables[6], key_value, other_key_value, root_first, root_second)
    got, root = lax.optimization_barrier((got, root))
    updated = finish(cores, keep, got, carry_next)

    next_window = jnp.where(slot == 7, fresh_frame, updated)
    arrived = [lax.ppermute(updated, FRAME, [(7, 2 * chip + 1)]) for chip in (1, 0, 2)]
    new_keys, new_values = insert_rows(
        after(root, updated), cache_keys, cache_values, offset
    )
    arrived, new_keys, new_values = lax.optimization_barrier((arrived, new_keys, new_values))
    finished = jnp.where(slot == 7, updated, arrived[0] + arrived[1] + arrived[2])
    finished = jnp.where(core == 0, lax.ppermute(finished, "core", [(1, 0)]), finished)
    return (next_window[None], finished, new_keys, new_values)


def solution(mesh):
    split = Mesh(mesh.devices.reshape(4, 2, 4, 2, 4), FRAME + FSDP)
    return jax.shard_map(
        step,
        mesh=split,
        in_specs=(
            P(FRAME, FSDP, None),
            P(FRAME),
            P(FRAME),
            P(),
            P(),
            P(),
            P(None, None, FSDP),
            P(FSDP, None),
            P(FRAME, FSDP),
            P(FRAME, FSDP),
            P(FSDP, None),
        ),
        out_specs=(P(FRAME, FSDP, None), P(FSDP, None), P(FRAME, FSDP), P(FRAME, FSDP)),
        check_vma=False,
    )
```
